128 devices in a mesh: seq: 16 (over x, z), head: 8 (over y, core).
Axes of the slice: x: 4, y: 4, z: 4, core: 2. Of those that a mesh axis runs over, the one named last changes fastest.
Arguments:
- tokens: bfloat16 [32768, 1024], P(('seq', 'head')), may hold values from -6 to 6
- norm_gain: float32 [1024], replicated, may hold values from 0.5 to 1.5
- w_qkv: bfloat16 [1024, 8, 384], P(None, 'head'), may hold values from -0.1875 to 0.1875
- w_mem_gates: bfloat16 [8, 3, 128], P('head'), may hold values from -0.5 to 0.5
- persist_keys: bfloat16 [16, 1024], P(None, 'head'), may hold values from -6 to 6
- persist_values: bfloat16 [16, 1024], P(None, 'head'), may hold values from -6 to 6
- alpha_bias: float32 [8], P('head'), may hold values from -8 to -2
- eta_bias: float32 [8], P('head'), may hold values from -1 to 3
- w_out: bfloat16 [1024, 1024], P('head'), may hold values from -0.1875 to 0.1875
- ffn_gain: float32 [1024], replicated, may hold values from 0.5 to 1.5
- w_gate: bfloat16 [1024, 2816], replicated, may hold values from -0.1875 to 0.1875
- w_up: bfloat16 [1024, 2816], replicated, may hold values from -0.1875 to 0.1875
- w_down: bfloat16 [2816, 1024], replicated, may hold values from -0.109375 to 0.109375
- segment_ids: int32 [32768], replicated, may hold values from 0 to 3, as said below
- block_table: int32 [512], replicated, may hold values from 0 to 511, as said below
Outputs:
- mixed: bfloat16 [32768, 1024], P(('seq', 'head'))
- kv_cache: bfloat16 [512, 64, 2048], P('seq', None, 'head')
The draws below stay inside these ranges and needn't reach their ends.
Inputs may be any that keep to these rules, and one draw needn't show every extreme that they name: `segment_ids`: segment numbers never fall along the stream and change only at multiples of 64 tokens; all 4 numbers occur, and one prompt holds exactly 16384 tokens. `block_table`: A permutation of the cache rows. Row r belongs to owner r // 32; the 32 blocks of each index of seq (blocks i * 32 to (i + 1) * 32 - 1) put exactly 2 blocks with every owner.
All inputs are finite; a program needn't handle non-finite values.
Results may differ from the reference program's by a relative error of at most 0.02.
Values may be sent and summed in bfloat16 or wider, within the bound.
A program may use at most 128 MiB of HBM per device.

```python
import jax
import jax.numpy as jnp
from jax import lax

D = 1024
H = 8
HD = 128
FF = 2816
PERS = 16
SPAN = 64
SEGS = 4
TOKENS = 32768
BLOCKS = 512
BPS = 32
PER_OWNER = 2
N_SEQ = 16


def draw_segment_ids(key, part):
    blocks = TOKENS // SPAN
    half = blocks // 2
    first_key, second_key = jax.random.split(jax.random.fold_in(key, 11))
    cuts = jnp.sort(jax.random.permutation(first_key, half - 1)[:SEGS - 2] + 1)
    bounds = jnp.concatenate([jnp.zeros((1,), jnp.int32), cuts.astype(jnp.int32), jnp.full((1,), half, jnp.int32)])
    others = bounds[1:] - bounds[:-1]
    spot = jax.random.randint(second_key, (), 1, SEGS - 1)
    pieces = []
    for place in range(SEGS):
        before = others[min(place, SEGS - 2)]
        after = others[max(place - 1, 0)]
        pieces.append(jnp.where(place < spot, before, jnp.where(place == spot, half, after)))
    lengths = jnp.stack(pieces).astype(jnp.int32)
    ends = jnp.cumsum(lengths)
    block_ids = jnp.arange(blocks, dtype=jnp.int32)
    numbers = jnp.sum((block_ids[:, None] >= ends[None, :SEGS - 1]).astype(jnp.int32), axis=1)
    return jnp.repeat(numbers, SPAN).astype(jnp.int32)


def draw_block_table(key, part):
    sender_keys = jax.random.split(jax.random.fold_in(key, 21), N_SEQ)
    owner_keys = jax.random.split(jax.random.fold_in(key, 22), N_SEQ)
    sender_perms = jax.vmap(lambda piece: jax.random.permutation(piece, BPS))(sender_keys)
    owner_perms = jax.vmap(lambda piece: jax.random.permutation(piece, BPS))(owner_keys)
    owners = sender_perms % N_SEQ
    copies = sender_perms // N_SEQ
    senders = jnp.arange(N_SEQ, dtype=jnp.int32)[:, None]
    local_rows = owner_perms[owners, senders * PER_OWNER + copies]
    return (owners * BPS + local_rows).reshape(-1).astype(jnp.int32)


def block_levels(key, shape, cuts, low, top_value):
    loudness, own = 1.0, jax.random.fold_in(key, 6)
    for dim, shards_of in cuts:
        heights = jnp.exp(jax.random.uniform(jax.random.fold_in(own, dim), (shards_of,), jnp.float32, low / len(cuts), top_value / len(cuts)))
        loudness = loudness * jnp.repeat(heights, shape[dim] // shards_of).reshape([-1 if axis == dim else 1 for axis in range(len(shape))])
    return loudness


def centred(key, extent, deviation, limit, cuts=(), held_as=jnp.bfloat16):
    drawn = jax.random.normal(key, extent, jnp.float32) * deviation
    if len(cuts) > 0:
        drawn = block_levels(key, extent, cuts, -0.22, 0.18) * drawn
    return jnp.clip(drawn, min=-limit, max=limit).astype(held_as)


def setup_inputs(seed: int = 0) -> dict:
    splits = jax.random.split(jax.random.key(seed), 16)
    return {
        "tokens": centred(splits[0], (TOKENS, D), 1.0, 6.0, ((0, 128),)),
        "norm_gain": jnp.clip(1.0 + 0.1 * jax.random.normal(splits[1], (D,), jnp.float32), 0.5, 1.5),
        "w_qkv": centred(splits[2], (D, H, 3 * HD), D ** -0.5, 0.1875, ((1, 8),)),
        "w_mem_gates": centred(splits[3], (H, 3, HD), HD ** -0.5, 0.5, ((0, 8),)),
        "persist_keys": centred(splits[4], (PERS, H * HD), 1.0, 6.0, ((1, 8),)),
        "persist_values": centred(splits[5], (PERS, H * HD), 1.0, 6.0, ((1, 8),)),
        "alpha_bias": jnp.clip(-8.0 + 6.0 * jax.random.uniform(splits[6], (H,), jnp.float32) ** block_levels(splits[6], (H,), ((0, 8),), -0.2, 0.2), -8.0, -2.0),
        "eta_bias": jnp.clip(-1.0 + 4.0 * jax.random.uniform(splits[7], (H,), jnp.float32) ** block_levels(splits[7], (H,), ((0, 8),), -0.2, 0.2), -1.0, 3.0),
        "w_out": centred(splits[8], (H * HD, D), (H * HD) ** -0.5, 0.1875, ((0, 8),)),
        "ffn_gain": jnp.clip(1.0 + 0.1 * jax.random.normal(splits[9], (D,), jnp.float32), 0.5, 1.5),
        "w_gate": centred(splits[10], (D, FF), D ** -0.5, 0.1875),
        "w_up": centred(splits[11], (D, FF), D ** -0.5, 0.1875),
        "w_down": centred(splits[12], (FF, D), FF ** -0.5, 0.109375),
        "segment_ids": draw_segment_ids(jax.random.fold_in(splits[15], 71), 0),
        "block_table": draw_block_table(jax.random.fold_in(splits[15], 71), 0),
    }


EPS = 1e-05
TINY = 1e-06
HIGH = lax.Precision.HIGHEST

def rms_scale(values, gain):
    return values * lax.rsqrt(lax.optimization_barrier(jnp.mean(values * values, axis=-1, keepdims=True)) + EPS) * gain

def rms_plain(values):
    return values * lax.rsqrt(lax.optimization_barrier(jnp.mean(values * values, axis=-1, keepdims=True)) + TINY)

def reference(tokens, norm_gain, w_qkv, w_mem_gates, persist_keys, persist_values, alpha_bias, eta_bias, w_out, ffn_gain, w_gate, w_up, w_down, segment_ids, block_table):
    resid = tokens.astype(jnp.float32)
    normed = rms_scale(resid, norm_gain).astype(jnp.bfloat16)
    projected = jnp.dot(normed, w_qkv.reshape(D, H * 3 * HD), preferred_element_type=jnp.float32)
    projected = projected.reshape(TOKENS, H, 3, HD)
    queries = rms_plain(projected[:, :, 0]) * HD ** (-0.5)
    keys = rms_plain(projected[:, :, 1]) * HD ** (-0.5)
    values = projected[:, :, 2]
    logits = jnp.einsum('thd,hgd->thg', values, w_mem_gates.astype(jnp.float32), precision=HIGH)
    theta = jax.nn.sigmoid(logits[..., 0]) / SPAN
    alpha = jax.nn.sigmoid(lax.optimization_barrier(jnp.mean(logits[..., 1].reshape(BLOCKS, SPAN, H), axis=1)) + alpha_bias)
    eta = jax.nn.sigmoid(lax.optimization_barrier(jnp.mean(logits[..., 2].reshape(BLOCKS, SPAN, H), axis=1)) + eta_bias)
    id_blocks = segment_ids.reshape(BLOCKS, SPAN)
    keep = jnp.concatenate([jnp.zeros((1,), jnp.float32), (id_blocks[1:, 0] == id_blocks[:-1, -1]).astype(jnp.float32)])
    pkeys = persist_keys.astype(jnp.float32).reshape(PERS, H, HD)
    pvals = persist_values.astype(jnp.float32).reshape(PERS, H, HD)
    initial = jnp.einsum('phd,phe->hde', pkeys, pvals, precision=HIGH) / PERS

    def span_step(carry, item):
        memory, moment = carry
        qry, key_rows, val_rows, weight, forget, carry_rate, kept = item
        held = kept * memory + (1.0 - kept) * initial
        moment_in = kept * moment
        recalled = jnp.einsum('thd,hde->the', qry, held, precision=HIGH)
        gram = jnp.einsum('th,thd,the->hde', weight, key_rows, key_rows, precision=HIGH)
        cross = jnp.einsum('th,thd,the->hde', weight, key_rows, val_rows, precision=HIGH)
        moment = carry_rate[:, None, None] * moment_in - jnp.einsum('hde,hef->hdf', gram, held, precision=HIGH) + cross
        memory = (1.0 - forget)[:, None, None] * held + moment
        return ((memory, moment), recalled)
    items = (queries.reshape(BLOCKS, SPAN, H, HD), keys.reshape(BLOCKS, SPAN, H, HD), values.reshape(BLOCKS, SPAN, H, HD), theta.reshape(BLOCKS, SPAN, H), alpha, eta, keep)
    start = jnp.zeros((H, HD, HD), jnp.float32)
    unused, recalled = lax.scan(span_step, (start, start), items)
    retrieved = rms_plain(recalled.reshape(TOKENS, H, HD)).astype(jnp.bfloat16).reshape(TOKENS, H * HD)
    residual = resid + jnp.dot(retrieved, w_out, preferred_element_type=jnp.float32)
    ffn_in = rms_scale(residual, ffn_gain).astype(jnp.bfloat16)
    gate = jnp.dot(ffn_in, w_gate, preferred_element_type=jnp.float32)
    upper = jnp.dot(ffn_in, w_up, preferred_element_type=jnp.float32)
    hidden = (jax.nn.silu(gate) * upper).astype(jnp.bfloat16)
    mixed = (residual + jnp.dot(hidden, w_down, preferred_element_type=jnp.float32)).astype(jnp.bfloat16)
    pairs = jnp.stack([keys, values], axis=2).astype(jnp.bfloat16).reshape(BLOCKS, SPAN, 2 * H * HD)
    kv_cache = jnp.zeros((BLOCKS, SPAN, 2 * H * HD), jnp.bfloat16).at[block_table].set(pairs)
    return (mixed, kv_cache)
```

```python
import jax
import jax.numpy as jnp
from jax import lax
from jax.experimental import pallas as pl
from jax.experimental.pallas import tpu as pltpu
from jax.sharding import PartitionSpec as P

D = 1024
HD = 128
FF = 2816
PERS = 16
SPAN = 64
ROWS = 256
BPS = 32
EPS = 1e-05
TINY = 1e-06
MIB = 1 << 20
MESH = pl.DeviceIdType.MESH
F32 = jnp.float32
BF16 = jnp.bfloat16


def sigmoid(x):
    return 1.0 / (1.0 + jnp.exp(-x))


def unit(x):
    return x * lax.rsqrt(jnp.mean(x * x, axis=-1, keepdims=True) + TINY)


def mm(a, b):
    return jnp.dot(a.astype(BF16), b.astype(BF16), preferred_element_type=F32)


def compose(later, earlier):
    joined = mm(later[:, :256], earlier)
    return joined[:, :256], joined[:, 256:] + later[:, 256:]


def layer_kernel(
    keep_ref, order_ref, ab_ref, eb_ref,
    tokens_ref, ngain_ref, wq_ref, wmg_ref, pk_ref, pv_ref, wout_ref, fgain_ref,
    wg_hbm, wu_hbm, wd_hbm,
    mixed_ref, kv_hbm,
    xg, wo, wg, wu, wd, kvbuf, kvsend, rm, rs, pt, gmap, pz, srow, sin, ysend, xin,
    retsend, ret, resid, acc, ffn_in,
    local_sem, kvl_sem, xs_sem, xy_sem, xc_sem, ws_sem, wy_sem, wc_sem,
    gs_sem, gr_sem, hs_sem, hr_sem, as_sem, ar_sem, ks_sem, kr_sem,
):
    seq = lax.axis_index("seq")
    head = lax.axis_index("head")
    sx, sz = seq // 4, seq % 4
    y, c = head // 2, head % 2
    up = ((y + 1) % 4) * 2 + c
    down = ((y + 3) % 4) * 2 + c
    twin = y * 2 + (1 - c)
    znext = sx * 4 + (sz + 1) % 4
    zprev = sx * 4 + (sz + 3) % 4
    xnext = ((sx + 1) % 4) * 4 + sz

    def remote(src, dst, ssem, rsem, s, h):
        return pltpu.make_async_remote_copy(
            src_ref=src, dst_ref=dst, send_sem=ssem, recv_sem=rsem, device_id=(s, h), device_id_type=MESH
        )

    loads = [
        pltpu.make_async_copy(wg_hbm, wg, local_sem.at[0]),
        pltpu.make_async_copy(wu_hbm, wu, local_sem.at[1]),
        pltpu.make_async_copy(wd_hbm, wd, local_sem.at[2]),
    ]

    barrier = pltpu.get_barrier_semaphore()

    def greet_head(o, _):
        pl.semaphore_signal(barrier, inc=1, device_id=(seq, (head + o) % 8), device_id_type=MESH)
        return 0

    def greet_seq(o, _):
        pl.semaphore_signal(barrier, inc=1, device_id=((seq + o) % 16, head), device_id_type=MESH)
        return 0

    lax.fori_loop(1, 8, greet_head, 0)
    lax.fori_loop(1, 16, greet_seq, 0)

    tok = tokens_ref[...].astype(F32)
    scale = lax.rsqrt(jnp.mean(tok * tok, axis=-1, keepdims=True) + EPS)
    xg[head] = (tok * scale * ngain_ref[...]).astype(BF16)

    pl.semaphore_wait(barrier, 22)

    mine = xg.at[head]
    x_twin = remote(mine, mine, xs_sem.at[0], xc_sem.at[0], seq, twin)
    x_up = remote(mine, mine, xs_sem.at[1], xy_sem.at[1], seq, up)
    x_down = remote(mine, mine, xs_sem.at[2], xy_sem.at[2], seq, down)
    x_up.start()
    x_down.start()
    x_twin.start()
    for load in loads:
        load.start()

    initial = jnp.dot(
        pk_ref[...].astype(F32).T.astype(BF16), pv_ref[...], preferred_element_type=F32
    ) * (1.0 / PERS)
    row = lax.broadcasted_iota(jnp.int32, (HD, 3 * HD), 0)
    col = lax.broadcasted_iota(jnp.int32, (HD, 3 * HD), 1)
    eye_m = (row == col).astype(F32)
    eye_s = (row + HD == col).astype(F32)
    zero_wide = jnp.zeros((HD, 2 * HD), F32)
    fresh = jnp.concatenate([zero_wide, initial], axis=1)
    zero_rows = jnp.zeros((SPAN, 2 * HD), F32)

    def arrive(p, _):
        off = jnp.where(p == 1, 3, jnp.where(p == 2, 1, jnp.where(p == 3, 2, 0)))
        yp = (y + off) % 4
        slot = xg.at[2 * yp + c]
        other = xg.at[2 * yp + 1 - c]

        @pl.when(p > 0)
        def _():
            remote(slot, slot, xs_sem.at[0], xy_sem.at[p], seq, up).wait_recv()

        @pl.when(p == 1)
        def _():
            half = xg.at[2 * yp + c, pl.ds(0, ROWS // 2)]
            remote(half, half, xs_sem.at[3], xy_sem.at[3], seq, up).start()

        @pl.when(p == 2)
        def _():
            half = xg.at[2 * yp + c, pl.ds(ROWS // 2, ROWS // 2)]
            remote(half, half, xs_sem.at[4], xy_sem.at[3], seq, down).start()

        @pl.when(p > 0)
        def _():
            remote(slot, slot, xs_sem.at[4 + p], xc_sem.at[p], seq, twin).start()

        remote(other, other, xs_sem.at[0], xc_sem.at[p], seq, twin).wait_recv()

        x = xg[pl.ds(2 * yp, 2)].reshape(2 * ROWS, D)
        proj = jnp.dot(x, wq_ref[...], preferred_element_type=F32)
        q = unit(proj[:, :HD]) * HD ** (-0.5)
        k = unit(proj[:, HD : 2 * HD]) * HD ** (-0.5)
        v = proj[:, 2 * HD :]
        wmg = wmg_ref[...].astype(F32)
        theta = sigmoid(jnp.sum(v * wmg[0:1], axis=-1, keepdims=True)) * (1.0 / SPAN)
        mean_v = jnp.mean(v.reshape(8, SPAN, HD), axis=1)
        alpha = sigmoid(jnp.sum(mean_v * wmg[1:2], axis=-1, keepdims=True) + ab_ref[0])
        eta = sigmoid(jnp.sum(mean_v * wmg[2:3], axis=-1, keepdims=True) + eb_ref[0])
        qb, kb = q.astype(BF16), k.astype(BF16)
        kvbuf[pl.ds(yp * 8, 8), :, :HD] = kb.reshape(8, SPAN, HD)
        kvbuf[pl.ds(yp * 8, 8), :, HD:] = v.astype(BF16).reshape(8, SPAN, HD)

        state = [(eye_m, eye_s), (eye_m, eye_s)]
        reads = [[], []]
        for step in range(4):
            for half in range(2):
                b = half * 4 + step
                rows = slice(b * SPAN, (b + 1) * SPAN)
                memory, moment = state[half]
                keep = keep_ref[yp * 8 + b]
                held = keep * memory + (1.0 - keep) * fresh
                both = mm(jnp.concatenate([qb[rows], kb[rows]], axis=0), held)
                reads[half].append(both[:SPAN])
                wide_v = jnp.concatenate([zero_rows, v[rows]], axis=1)
                push = theta[rows] * (wide_v - both[SPAN:])
                moment = eta[b : b + 1] * (keep * moment) + mm(k[rows].T, push)
                memory = (1.0 - alpha[b : b + 1]) * held + moment
                state[half] = (memory, moment)
        even = jnp.concatenate(state[0], axis=0)
        odd = jnp.concatenate(state[1], axis=0)
        tmap, tshift = compose(odd, even)
        pt[yp, :, :256] = tmap
        pt[yp, :, 256:] = tshift
        read_even = jnp.concatenate(reads[0], axis=0)
        read_odd = jnp.concatenate(reads[1], axis=0)
        omap, oshift = compose(read_odd, even)
        rm[2 * yp] = read_even[:, :256].astype(BF16)
        rs[2 * yp] = read_even[:, 256:]
        rm[2 * yp + 1] = omap.astype(BF16)
        rs[2 * yp + 1] = oshift
        return 0

    lax.fori_loop(0, 4, arrive, 0)

    def join(later, earlier):
        return jnp.concatenate(compose(later, earlier), axis=1)

    first = join(pt[1], pt[0])
    total = join(join(pt[3], pt[2]), first)
    gmap[sz] = total.astype(BF16)
    gmine = gmap.at[sz]
    remote(gmine, gmine, gs_sem.at[0], gr_sem.at[1], znext, head).start()
    remote(gmine, gmine, gs_sem.at[1], gr_sem.at[2], zprev, head).start()

    wo[head] = wout_ref[...]
    wmine = wo.at[head]
    remote(wmine, wmine, ws_sem.at[1], wy_sem.at[1], seq, up).start()
    remote(wmine, wmine, ws_sem.at[2], wy_sem.at[2], seq, down).start()
    remote(wmine, wmine, ws_sem.at[0], wc_sem.at[0], seq, twin).start()

    def fold(p, emap):
        read = rm[pl.ds(2 * p, 2)].reshape(2 * ROWS, 2 * HD)
        out = jnp.dot(read, emap.astype(BF16), preferred_element_type=F32)
        rm[pl.ds(2 * p, 2)] = out[:, :256].astype(BF16).reshape(2, ROWS, 2 * HD)
        rs[pl.ds(2 * p, 2)] = rs[pl.ds(2 * p, 2)] + out[:, 256:].reshape(2, ROWS, HD)

    fold(1, pt[0])
    fold(2, first)
    fold(3, join(pt[2], first))

    def place(p, _):
        kvsend[p] = kvbuf[order_ref[p]]
        return 0

    lax.fori_loop(0, BPS, place, 0)

    def gslot(step):
        return gmap.at[(sz + step) % 4]

    remote(gslot(3), gslot(3), gs_sem.at[0], gr_sem.at[1], znext, head).wait_recv()
    half = gmap.at[(sz + 3) % 4, pl.ds(0, 128)]
    remote(half, half, gs_sem.at[2], gr_sem.at[3], znext, head).start()
    remote(gslot(1), gslot(1), gs_sem.at[0], gr_sem.at[2], znext, head).wait_recv()
    half = gmap.at[(sz + 1) % 4, pl.ds(128, 128)]
    remote(half, half, gs_sem.at[3], gr_sem.at[3], zprev, head).start()
    remote(gslot(2), gslot(2), gs_sem.at[0], gr_sem.at[3], znext, head).wait_recv()

    def bjoin(later, earlier):
        tmap, tshift = compose(later.astype(F32), earlier)
        return jnp.concatenate([tmap, tshift], axis=1)

    low = bjoin(gmap[1], gmap[0])
    total = join(bjoin(gmap[3], gmap[2]), low)
    srow[...] = total[:, 256:].astype(BF16)
    remote(srow, sin, hs_sem.at[0], hr_sem.at[0], xnext, head).start()

    @pl.when(sz == 1)
    def _():
        pz[...] = gmap[0]

    @pl.when(sz == 2)
    def _():
        pz[...] = low.astype(BF16)

    @pl.when(sz == 3)
    def _():
        pz[...] = bjoin(gmap[2], low).astype(BF16)

    wprev, wnext = wo.at[((y + 3) % 4) * 2 + c], wo.at[((y + 1) % 4) * 2 + c]
    remote(wprev, wprev, ws_sem.at[1], wy_sem.at[1], seq, up).wait_recv()
    half = wo.at[((y + 3) % 4) * 2 + c, pl.ds(0, 64)]
    remote(half, half, ws_sem.at[3], wy_sem.at[3], seq, up).start()
    remote(wprev, wprev, ws_sem.at[5], wc_sem.at[1], seq, twin).start()
    remote(wnext, wnext, ws_sem.at[1], wy_sem.at[2], seq, up).wait_recv()
    half = wo.at[((y + 1) % 4) * 2 + c, pl.ds(64, 64)]
    remote(half, half, ws_sem.at[4], wy_sem.at[3], seq, down).start()
    remote(wnext, wnext, ws_sem.at[6], wc_sem.at[2], seq, twin).start()

    remote(srow, sin, hs_sem.at[0], hr_sem.at[0], xnext, head).wait_recv()
    ysend[...] = (mm(total[:, :256], sin[...]) + total[:, 256:]).astype(BF16)
    remote(ysend, xin, hs_sem.at[1], hr_sem.at[1], xnext, head).start()

    @pl.when(sz > 0)
    def _():
        def fold_all(p, _):
            fold(p, pz[...])
            return 0

        lax.fori_loop(0, 4, fold_all, 0)

    def kv_copy(o):
        to = (seq + o) % 16
        return remote(
            kvsend.at[pl.ds(2 * to, 2)], kv_hbm.at[pl.ds(2 * seq, 2)], ks_sem.at[o], kr_sem.at[o], to, head
        )

    def kv_arrival(o):
        source = (seq + 16 - o) % 16
        return remote(
            kvsend.at[pl.ds(2 * source, 2)], kv_hbm.at[pl.ds(2 * source, 2)], ks_sem.at[o], kr_sem.at[o], source, head
        )

    def kv_start(o, _):
        kv_copy(o).start()
        return 0

    lax.fori_loop(1, 16, kv_start, 0)
    kv_own = pltpu.make_async_copy(kvsend.at[pl.ds(2 * seq, 2)], kv_hbm.at[pl.ds(2 * seq, 2)], kvl_sem)
    kv_own.start()

    wfar = wo.at[((y + 2) % 4) * 2 + c]
    remote(wfar, wfar, ws_sem.at[1], wy_sem.at[3], seq, up).wait_recv()
    remote(wfar, wfar, ws_sem.at[7], wc_sem.at[3], seq, twin).start()

    remote(ysend, xin, hs_sem.at[1], hr_sem.at[1], xnext, head).wait_recv()
    enter = xin[...]

    def answer(j):
        recalled = jnp.dot(rm[j], enter, preferred_element_type=F32) + rs[j]
        return unit(recalled).astype(BF16)

    def ret_copy(oy, oc):
        o = oy * 2 + oc
        to = ((y + oy) % 4) * 2 + (c + oc) % 2
        return remote(retsend.at[o], ret.at[head], as_sem.at[o], ar_sem.at[o], seq, to)

    def ret_arrival(oy, oc):
        o = oy * 2 + oc
        source = ((y + 4 - oy) % 4) * 2 + (c + oc) % 2
        return remote(retsend.at[o], ret.at[source], as_sem.at[o], ar_sem.at[o], seq, source)

    turns = [(2, 0), (2, 1), (1, 0), (1, 1), (3, 0), (3, 1), (0, 1)]
    for oy, oc in turns:
        retsend[oy * 2 + oc] = answer(((y + oy) % 4) * 2 + (c + oc) % 2)
        ret_copy(oy, oc).start()
    ret[head] = answer(head)

    for p, off in ((0, 0), (1, 3), (2, 1), (3, 2)):
        other = wo.at[((y + off) % 4) * 2 + 1 - c]
        remote(other, other, ws_sem.at[0], wc_sem.at[p], seq, twin).wait_recv()
    for load in loads:
        load.wait()
    for oy, oc in turns:
        ret_arrival(oy, oc).wait_recv()

    total = tokens_ref[...].astype(F32)
    for i in range(4):
        left = jnp.concatenate([ret[2 * i], ret[2 * i + 1]], axis=1)
        total = total + jnp.dot(left, wo[2 * i : 2 * i + 2].reshape(2 * HD, D), preferred_element_type=F32)
    acc[...] = total
    scale = lax.rsqrt(jnp.mean(total * total, axis=-1, keepdims=True) + EPS)
    ffn_in[...] = (total * scale * fgain_ref[...]).astype(BF16)

    def ffn(t, _):
        cols = pl.ds(pl.multiple_of(t * 256, 256), 256)
        gate = jnp.dot(ffn_in[...], wg[:, cols], preferred_element_type=F32)
        upper = jnp.dot(ffn_in[...], wu[:, cols], preferred_element_type=F32)
        hidden = (gate / (1.0 + jnp.exp(-gate)) * upper).astype(BF16)
        acc[...] += jnp.dot(hidden, wd[cols, :], preferred_element_type=F32)
        return 0

    lax.fori_loop(0, FF // 256, ffn, 0)
    mixed_ref[...] = acc[...].astype(BF16)

    def kv_end(o, _):
        kv_arrival(o).wait_recv()
        kv_copy(o).wait_send()
        return 0

    lax.fori_loop(1, 16, kv_end, 0)
    kv_own.wait()
    whole = xg.at[head]
    for i in (0, 1, 2, 5, 6, 7):
        remote(whole, whole, xs_sem.at[i], xy_sem.at[1], seq, up).wait_send()
    half = xg.at[head, pl.ds(0, ROWS // 2)]
    for i in (3, 4):
        remote(half, half, xs_sem.at[i], xy_sem.at[1], seq, up).wait_send()
    for i in (0, 1, 2, 5, 6, 7):
        remote(wmine, wmine, ws_sem.at[i], wy_sem.at[1], seq, up).wait_send()
    half = wo.at[head, pl.ds(0, 64)]
    for i in (3, 4):
        remote(half, half, ws_sem.at[i], wy_sem.at[1], seq, up).wait_send()
    for i in (0, 1):
        remote(gmine, gmine, gs_sem.at[i], gr_sem.at[1], znext, head).wait_send()
    half = gmap.at[sz, pl.ds(0, 128)]
    for i in (2, 3):
        remote(half, half, gs_sem.at[i], gr_sem.at[1], znext, head).wait_send()
    remote(srow, sin, hs_sem.at[0], hr_sem.at[0], xnext, head).wait_send()
    remote(ysend, xin, hs_sem.at[1], hr_sem.at[1], xnext, head).wait_send()
    for oy, oc in turns:
        ret_copy(oy, oc).wait_send()


def per_device(
    tokens, norm_gain, w_qkv, w_mem_gates, persist_keys, persist_values, alpha_bias, eta_bias,
    w_out, ffn_gain, w_gate, w_up, w_down, segment_ids, block_table,
):
    seq = lax.axis_index("seq")
    ids = segment_ids.reshape(-1, SPAN)[:, 0]
    keep_all = jnp.concatenate([jnp.zeros((1,), F32), (ids[1:] == ids[:-1]).astype(F32)])
    keep = lax.dynamic_slice_in_dim(keep_all, seq * BPS, BPS)
    slots = jnp.arange(BPS, dtype=jnp.int32)
    mine = lax.dynamic_slice_in_dim(block_table, seq * BPS, BPS)
    place = (mine // BPS) * BPS + slots
    position = jnp.sum((place[None, :] < place[:, None]).astype(jnp.int32), axis=1)
    order = jnp.sum(jnp.where(position[None, :] == slots[:, None], slots[None, :], 0), axis=1)

    vmem = pl.BlockSpec(memory_space=pltpu.VMEM)
    smem = pl.BlockSpec(memory_space=pltpu.SMEM)
    anywhere = pl.BlockSpec(memory_space=pl.ANY)
    dma = pltpu.SemaphoreType.DMA
    mixed, arrived = pl.pallas_call(
        layer_kernel,
        out_shape=(
            jax.ShapeDtypeStruct((ROWS, D), BF16),
            jax.ShapeDtypeStruct((BPS, SPAN, 2 * HD), BF16),
        ),
        in_specs=[smem] * 4 + [vmem] * 8 + [anywhere] * 3,
        out_specs=(vmem, anywhere),
        scratch_shapes=[
            pltpu.VMEM((8, ROWS, D), BF16),
            pltpu.VMEM((8, HD, D), BF16),
            pltpu.VMEM((D, FF), BF16),
            pltpu.VMEM((D, FF), BF16),
            pltpu.VMEM((FF, D), BF16),
            pltpu.VMEM((BPS, SPAN, 2 * HD), BF16),
            pltpu.VMEM((BPS, SPAN, 2 * HD), BF16),
            pltpu.VMEM((8, ROWS, 2 * HD), BF16),
            pltpu.VMEM((8, ROWS, HD), F32),
            pltpu.VMEM((4, 2 * HD, 3 * HD), F32),
            pltpu.VMEM((4, 2 * HD, 3 * HD), BF16),
            pltpu.VMEM((2 * HD, 3 * HD), BF16),
            pltpu.VMEM((2 * HD, HD), BF16),
            pltpu.VMEM((2 * HD, HD), BF16),
            pltpu.VMEM((2 * HD, HD), BF16),
            pltpu.VMEM((2 * HD, HD), BF16),
            pltpu.VMEM((8, ROWS, HD), BF16),
            pltpu.VMEM((8, ROWS, HD), BF16),
            pltpu.VMEM((8, HD), F32),
            pltpu.VMEM((ROWS, D), F32),
            pltpu.VMEM((ROWS, D), BF16),
            dma((3,)), dma,
            dma((8,)), dma((4,)), dma((4,)),
            dma((8,)), dma((4,)), dma((4,)),
            dma((4,)), dma((4,)),
            dma((2,)), dma((2,)),
            dma((8,)), dma((8,)),
            dma((16,)), dma((16,)),
        ],
        compiler_params=pltpu.CompilerParams(
            collective_id=0, has_side_effects=True, vmem_limit_bytes=56 * MIB
        ),
    )(
        keep, order, alpha_bias, eta_bias,
        tokens, norm_gain.reshape(1, D), w_qkv.reshape(D, 3 * HD), w_mem_gates.reshape(3, HD),
        persist_keys, persist_values, w_out, ffn_gain.reshape(1, D),
        w_gate, w_up, w_down,
    )

    wanted = seq * BPS + slots
    blocks = jnp.arange(block_table.shape[0], dtype=jnp.int32)
    block_of = jnp.sum(jnp.where(block_table[None, :] == wanted[:, None], blocks[None, :], 0), axis=1)
    spot = jnp.sum((block_of[None, :] < block_of[:, None]).astype(jnp.int32), axis=1)
    return mixed, arrived[spot]


def solution(mesh):
    return jax.shard_map(
        per_device,
        mesh=mesh,
        in_specs=(
            P(("seq", "head"), None),
            P(),
            P(None, "head", None),
            P("head", None, None),
            P(None, "head"),
            P(None, "head"),
            P("head"),
            P("head"),
            P("head", None),
            P(),
            P(),
            P(),
            P(),
            P(),
            P(),
        ),
        out_specs=(P(("seq", "head"), None), P("seq", None, "head")),
        check_vma=False,
    )
```

```python
import jax
import jax.numpy as jnp
from jax import lax
from jax.experimental import pallas as pl
from jax.experimental.pallas import tpu as pltpu
from jax.sharding import PartitionSpec as P

D = 1024
HD = 128
FF = 2816
PERS = 16
SPAN = 64
ROWS = 256
PIECE = 64
TOKENS = 32768
BPS = 32
EPS = 1e-05
TINY = 1e-06
MIB = 1 << 20
MESH = pl.DeviceIdType.MESH
F32 = jnp.float32
BF16 = jnp.bfloat16


def sigmoid(x):
    return 1.0 / (1.0 + jnp.exp(-x))


def unit(x):
    return x * lax.rsqrt(jnp.mean(x * x, axis=-1, keepdims=True) + TINY)


def mm(a, b):
    return jnp.dot(a.astype(BF16), b.astype(BF16), preferred_element_type=F32)


def compose(later, earlier):
    joined = mm(later[:, :256], earlier)
    return joined[:, :256], joined[:, 256:] + later[:, 256:]


def layer_kernel(
    ab_ref, eb_ref, table_ref, ids_hbm,
    wide_table_ref, tokens_ref, ngain_ref, wq_ref, wmg_ref, pk_ref, pv_ref, wout_ref, fgain_ref,
    wg_hbm, wu_hbm, wd_hbm,
    mixed_ref, kv_hbm, rowof_ref,
    ids, before, order, xg, wo, wg, wu, wd, kvbuf, kvsend, rm, rs, pt, gmap, pz, srow, sin, ysend, xin,
    retsend, ret, resid, ffn_in, hid,
    local_sem, kvl_sem, own_sem, fwd_sem, tws_sem, yr_sem, twr_sem, ws_sem, wy_sem, wc_sem,
    gs_sem, gr_sem, hs_sem, hr_sem, as_sem, ar_sem, ks_sem, kr_sem,
):
    seq = lax.axis_index("seq")
    head = lax.axis_index("head")
    sx, sz = seq // 4, seq % 4
    y, c = head // 2, head % 2
    up = ((y + 1) % 4) * 2 + c
    down = ((y + 3) % 4) * 2 + c
    twin = y * 2 + (1 - c)
    znext = sx * 4 + (sz + 1) % 4
    zprev = sx * 4 + (sz + 3) % 4
    xnext = ((sx + 1) % 4) * 4 + sz

    def remote(src, dst, ssem, rsem, s, h):
        return pltpu.make_async_remote_copy(
            src_ref=src, dst_ref=dst, send_sem=ssem, recv_sem=rsem, device_id=(s, h), device_id_type=MESH
        )

    loads = [
        pltpu.make_async_copy(wg_hbm, wg, local_sem.at[0]),
        pltpu.make_async_copy(wu_hbm, wu, local_sem.at[1]),
        pltpu.make_async_copy(wd_hbm, wd, local_sem.at[2]),
    ]
    mine_ids = pl.multiple_of(seq * (BPS * SPAN), 1024)
    prior_ids = pl.multiple_of((seq * (BPS * SPAN) + TOKENS - 1024) % TOKENS, 1024)
    id_loads = [
        pltpu.make_async_copy(ids_hbm.at[pl.ds(mine_ids, BPS * SPAN)], ids, local_sem.at[3]),
        pltpu.make_async_copy(ids_hbm.at[pl.ds(prior_ids, 1024)], before, local_sem.at[4]),
    ]
    for load in id_loads:
        load.start()

    barrier = pltpu.get_barrier_semaphore()

    def greet_head(o, _):
        pl.semaphore_signal(barrier, inc=1, device_id=(seq, (head + o) % 8), device_id_type=MESH)
        return 0

    def greet_seq(o, _):
        pl.semaphore_signal(barrier, inc=1, device_id=((seq + o) % 16, head), device_id_type=MESH)
        return 0

    lax.fori_loop(1, 8, greet_head, 0)
    lax.fori_loop(1, 16, greet_seq, 0)

    tok = tokens_ref[...].astype(F32)
    scale = lax.rsqrt(jnp.mean(tok * tok, axis=-1, keepdims=True) + EPS)
    xg[head] = (tok * scale * ngain_ref[...]).astype(BF16)

    pl.semaphore_wait(barrier, 22)

    def piece(slot, i):
        return xg.at[slot, pl.ds(i * PIECE, PIECE)]

    def y_copy(slot, i, sem, kind, to):
        part = piece(slot, i)
        return remote(part, part, sem, yr_sem.at[kind, i], seq, to)

    def twin_copy(slot, i, kind):
        part = piece(slot, i)
        return remote(part, part, tws_sem.at[kind, i], twr_sem.at[kind, i], seq, twin)

    slots = [2 * ((y + off) % 4) + c for off in (0, 3, 1, 2)]
    others = [2 * ((y + off) % 4) + 1 - c for off in (0, 3, 1, 2)]
    for i in range(4):
        y_copy(head, i, own_sem.at[0, i], 1, up).start()
        y_copy(head, 3 - i, own_sem.at[1, 3 - i], 2, down).start()
    for i in range(4):
        twin_copy(head, i, 0).start()
    for load in loads:
        load.start()

    initial = jnp.dot(
        pk_ref[...].astype(F32).T.astype(BF16), pv_ref[...], preferred_element_type=F32
    ) * (1.0 / PERS)
    row = lax.broadcasted_iota(jnp.int32, (HD, 3 * HD), 0)
    col = lax.broadcasted_iota(jnp.int32, (HD, 3 * HD), 1)
    eye_m = (row == col).astype(F32)
    eye_s = (row + HD == col).astype(F32)
    zero_wide = jnp.zeros((HD, 2 * HD), F32)
    fresh = jnp.concatenate([zero_wide, initial], axis=1)
    zero_rows = jnp.zeros((SPAN, 2 * HD), F32)

    wide = wide_table_ref[...]
    place_no = lax.broadcasted_iota(jnp.int32, (4, 128), 0) * 128 + lax.broadcasted_iota(jnp.int32, (4, 128), 1)
    owner_no = lax.shift_right_logical(wide, 5)
    key_no = owner_no * BPS + (place_no & (BPS - 1))
    position = jnp.zeros((4, 128), jnp.int32)
    for i in range(BPS):
        one = lax.shift_right_logical(table_ref[seq * BPS + i], 5) * BPS + i
        position = position + (one < key_no).astype(jnp.int32)
    position = jnp.where(lax.shift_right_logical(place_no, 5) == seq, position, -1)
    owned = (owner_no == seq).astype(F32)
    earlier = lax.broadcasted_iota(jnp.int32, (128, 128), 0) < lax.broadcasted_iota(jnp.int32, (128, 128), 1)
    rank = mm(jnp.concatenate([owned, owned], axis=0), earlier.astype(F32))[:4]
    rank = rank + 8.0 * lax.broadcasted_iota(jnp.int32, (4, 128), 0).astype(F32)
    rank = jnp.where(owned > 0.0, rank, -1.0)
    for i in range(BPS):
        order[i] = jnp.sum(jnp.where(position == i, place_no & (BPS - 1), 0))
        rowof_ref[i] = jnp.sum(jnp.where(rank == float(i), wide & (BPS - 1), 0))
    for load in id_loads:
        load.wait()

    def keep_of(yp, b):
        block = yp * 8 + b
        here = ids[block * SPAN]
        there = ids[jnp.maximum(block * SPAN - 1, 0)]
        there = jnp.where(block == 0, before[1023], there)
        there = jnp.where(block + seq == 0, -1, there)
        return jnp.where(here == there, 1.0, 0.0)

    def process(chips):
        work = []
        for yp in chips:
            x = xg[pl.ds(2 * yp, 2)].reshape(2 * ROWS, D)
            proj = jnp.dot(x, wq_ref[...], preferred_element_type=F32)
            q = unit(proj[:, :HD]) * HD ** (-0.5)
            k = unit(proj[:, HD : 2 * HD]) * HD ** (-0.5)
            v = proj[:, 2 * HD :]
            wmg = wmg_ref[...].astype(F32)
            theta = sigmoid(jnp.sum(v * wmg[0:1], axis=-1, keepdims=True)) * (1.0 / SPAN)
            mean_v = jnp.mean(v.reshape(8, SPAN, HD), axis=1)
            alpha = sigmoid(jnp.sum(mean_v * wmg[1:2], axis=-1, keepdims=True) + ab_ref[0])
            eta = sigmoid(jnp.sum(mean_v * wmg[2:3], axis=-1, keepdims=True) + eb_ref[0])
            qb, kb = q.astype(BF16), k.astype(BF16)
            kvbuf[pl.ds(yp * 8, 8), :, :HD] = kb.reshape(8, SPAN, HD)
            kvbuf[pl.ds(yp * 8, 8), :, HD:] = v.astype(BF16).reshape(8, SPAN, HD)
            for half in range(2):
                work.append([yp, half * 4, qb, k, kb, v, theta, alpha, eta, eye_m, eye_s, []])
        for step in range(4):
            for item in work:
                yp, first_block, qb, k, kb, v, theta, alpha, eta, memory, moment, reads = item
                b = first_block + step
                rows = slice(b * SPAN, (b + 1) * SPAN)
                keep = keep_of(yp, b)
                held = keep * memory + (1.0 - keep) * fresh
                both = mm(jnp.concatenate([qb[rows], kb[rows]], axis=0), held)
                reads.append(both[:SPAN])
                wide_v = jnp.concatenate([zero_rows, v[rows]], axis=1)
                push = theta[rows] * (wide_v - both[SPAN:])
                moment = eta[b : b + 1] * (keep * moment) + mm(k[rows].T, push)
                memory = (1.0 - alpha[b : b + 1]) * held + moment
                item[9], item[10] = memory, moment
        for i in range(0, len(work), 2):
            yp = work[i][0]
            even = jnp.concatenate([work[i][9], work[i][10]], axis=0)
            odd = jnp.concatenate([work[i + 1][9], work[i + 1][10]], axis=0)
            tmap, tshift = compose(odd, even)
            pt[yp, :, :256] = tmap
            pt[yp, :, 256:] = tshift
            read_even = jnp.concatenate(work[i][11], axis=0)
            read_odd = jnp.concatenate(work[i + 1][11], axis=0)
            omap, oshift = compose(read_odd, even)
            rm[2 * yp] = read_even[:, :256].astype(BF16)
            rs[2 * yp] = read_even[:, 256:]
            rm[2 * yp + 1] = omap.astype(BF16)
            rs[2 * yp + 1] = oshift

    def twin_in(kind):
        for i in range(4):
            twin_copy(others[kind], i, kind).wait_recv()

    twin_in(0)
    process([y])
    for i in range(4):
        y_copy(slots[1], i, own_sem.at[0, 0], 1, up).wait_recv()
        if i < 2:
            y_copy(slots[1], i, fwd_sem.at[i], 3, up).start()
        twin_copy(slots[1], i, 1).start()
        y_copy(slots[2], 3 - i, own_sem.at[0, 0], 2, up).wait_recv()
        if i < 2:
            y_copy(slots[2], 3 - i, fwd_sem.at[3 - i], 3, down).start()
        twin_copy(slots[2], 3 - i, 2).start()
    twin_in(1)
    twin_in(2)
    process([(y + 3) % 4, (y + 1) % 4])
    for i in (0, 3, 1, 2):
        y_copy(slots[3], i, own_sem.at[0, 0], 3, up).wait_recv()
        twin_copy(slots[3], i, 3).start()
    twin_in(3)
    process([(y + 2) % 4])

    def join(later, earlier):
        return jnp.concatenate(compose(later, earlier), axis=1)

    first = join(pt[1], pt[0])
    total = join(join(pt[3], pt[2]), first)
    gmap[sz] = total.astype(BF16)
    def g_copy(step, i, sem, kind, to):
        part = gmap.at[(sz + step) % 4, pl.ds(i * HD, HD)]
        return remote(part, part, sem, gr_sem.at[kind, i], to, head)

    for i in range(2):
        g_copy(0, i, gs_sem.at[0, i], 1, znext).start()
        g_copy(0, 1 - i, gs_sem.at[1, 1 - i], 2, zprev).start()

    wo[head] = wout_ref[...]
    wmine = wo.at[head]
    remote(wmine, wmine, ws_sem.at[1], wy_sem.at[1], seq, up).start()
    remote(wmine, wmine, ws_sem.at[2], wy_sem.at[2], seq, down).start()
    remote(wmine, wmine, ws_sem.at[0], wc_sem.at[0], seq, twin).start()

    def fold(p, emap):
        read = rm[pl.ds(2 * p, 2)].reshape(2 * ROWS, 2 * HD)
        out = jnp.dot(read, emap.astype(BF16), preferred_element_type=F32)
        rm[pl.ds(2 * p, 2)] = out[:, :256].astype(BF16).reshape(2, ROWS, 2 * HD)
        rs[pl.ds(2 * p, 2)] = rs[pl.ds(2 * p, 2)] + out[:, 256:].reshape(2, ROWS, HD)

    fold(1, pt[0])
    fold(2, first)
    fold(3, join(pt[2], first))

    def place(p, _):
        kvsend[p] = kvbuf[order[p]]
        return 0

    lax.fori_loop(0, BPS, place, 0)

    g_copy(3, 0, gs_sem.at[0, 0], 1, znext).wait_recv()
    g_copy(3, 0, gs_sem.at[2, 0], 3, znext).start()
    g_copy(1, 1, gs_sem.at[0, 0], 2, znext).wait_recv()
    g_copy(1, 1, gs_sem.at[2, 1], 3, zprev).start()
    g_copy(3, 1, gs_sem.at[0, 0], 1, znext).wait_recv()
    g_copy(1, 0, gs_sem.at[0, 0], 2, znext).wait_recv()
    g_copy(2, 0, gs_sem.at[0, 0], 3, znext).wait_recv()
    g_copy(2, 1, gs_sem.at[0, 0], 3, znext).wait_recv()

    def bjoin(later, earlier):
        tmap, tshift = compose(later.astype(F32), earlier)
        return jnp.concatenate([tmap, tshift], axis=1)

    low = bjoin(gmap[1], gmap[0])
    total = join(bjoin(gmap[3], gmap[2]), low)
    srow[...] = total[:, 256:].astype(BF16)
    remote(srow, sin, hs_sem.at[0], hr_sem.at[0], xnext, head).start()

    @pl.when(sz == 1)
    def _():
        pz[...] = gmap[0]

    @pl.when(sz == 2)
    def _():
        pz[...] = low.astype(BF16)

    @pl.when(sz == 3)
    def _():
        pz[...] = bjoin(gmap[2], low).astype(BF16)

    wprev, wnext = wo.at[((y + 3) % 4) * 2 + c], wo.at[((y + 1) % 4) * 2 + c]
    remote(wprev, wprev, ws_sem.at[1], wy_sem.at[1], seq, up).wait_recv()
    half = wo.at[((y + 3) % 4) * 2 + c, pl.ds(0, 64)]
    remote(half, half, ws_sem.at[3], wy_sem.at[3], seq, up).start()
    remote(wprev, wprev, ws_sem.at[5], wc_sem.at[1], seq, twin).start()
    remote(wnext, wnext, ws_sem.at[1], wy_sem.at[2], seq, up).wait_recv()
    half = wo.at[((y + 1) % 4) * 2 + c, pl.ds(64, 64)]
    remote(half, half, ws_sem.at[4], wy_sem.at[3], seq, down).start()
    remote(wnext, wnext, ws_sem.at[6], wc_sem.at[2], seq, twin).start()

    remote(srow, sin, hs_sem.at[0], hr_sem.at[0], xnext, head).wait_recv()
    ysend[...] = (mm(total[:, :256], sin[...]) + total[:, 256:]).astype(BF16)
    remote(ysend, xin, hs_sem.at[1], hr_sem.at[1], xnext, head).start()

    @pl.when(sz > 0)
    def _():
        def fold_all(p, _):
            fold(p, pz[...])
            return 0

        lax.fori_loop(0, 4, fold_all, 0)

    def kv_copy(o):
        to = (seq + o) % 16
        return remote(
            kvsend.at[pl.ds(2 * to, 2)], kv_hbm.at[pl.ds(2 * seq, 2)], ks_sem.at[o], kr_sem.at[o], to, head
        )

    def kv_arrival(o):
        source = (seq + 16 - o) % 16
        return remote(
            kvsend.at[pl.ds(2 * source, 2)], kv_hbm.at[pl.ds(2 * source, 2)], ks_sem.at[o], kr_sem.at[o], source, head
        )

    def kv_start(o, _):
        kv_copy(o).start()
        return 0

    lax.fori_loop(1, 16, kv_start, 0)
    kv_own = pltpu.make_async_copy(kvsend.at[pl.ds(2 * seq, 2)], kv_hbm.at[pl.ds(2 * seq, 2)], kvl_sem)
    kv_own.start()

    wfar = wo.at[((y + 2) % 4) * 2 + c]
    remote(wfar, wfar, ws_sem.at[1], wy_sem.at[3], seq, up).wait_recv()
    remote(wfar, wfar, ws_sem.at[7], wc_sem.at[3], seq, twin).start()

    remote(ysend, xin, hs_sem.at[1], hr_sem.at[1], xnext, head).wait_recv()
    enter = xin[...]

    def answer(j):
        recalled = jnp.dot(rm[j], enter, preferred_element_type=F32) + rs[j]
        return unit(recalled).astype(BF16)

    def ret_copy(oy, oc):
        o = oy * 2 + oc
        to = ((y + oy) % 4) * 2 + (c + oc) % 2
        return remote(retsend.at[o], ret.at[head], as_sem.at[o], ar_sem.at[o], seq, to)

    def ret_arrival(oy, oc):
        o = oy * 2 + oc
        source = ((y + 4 - oy) % 4) * 2 + (c + oc) % 2
        return remote(retsend.at[o], ret.at[source], as_sem.at[o], ar_sem.at[o], seq, source)

    turns = [(2, 0), (2, 1), (1, 0), (1, 1), (3, 0), (3, 1), (0, 1)]
    for oy, oc in turns:
        retsend[oy * 2 + oc] = answer(((y + oy) % 4) * 2 + (c + oc) % 2)
        ret_copy(oy, oc).start()
    ret[head] = answer(head)

    for p, off in ((0, 0), (1, 3), (2, 1), (3, 2)):
        other = wo.at[((y + off) % 4) * 2 + 1 - c]
        remote(other, other, ws_sem.at[0], wc_sem.at[p], seq, twin).wait_recv()
    for load in loads:
        load.wait()
    for oy, oc in turns:
        ret_arrival(oy, oc).wait_recv()

    total = tokens_ref[...].astype(F32)
    for i in range(4):
        left = jnp.concatenate([ret[2 * i], ret[2 * i + 1]], axis=1)
        total = total + jnp.dot(left, wo[2 * i : 2 * i + 2].reshape(2 * HD, D), preferred_element_type=F32)
    resid[...] = total
    scale = lax.rsqrt(jnp.mean(total * total, axis=-1, keepdims=True) + EPS)
    ffn_in[...] = (total * scale * fgain_ref[...]).astype(BF16)

    def widen(t, _):
        cols = pl.ds(pl.multiple_of(t * 256, 256), 256)
        gate = jnp.dot(ffn_in[...], wg[:, cols], preferred_element_type=F32)
        upper = jnp.dot(ffn_in[...], wu[:, cols], preferred_element_type=F32)
        hid[:, cols] = (gate / (1.0 + jnp.exp(-gate)) * upper).astype(BF16)
        return 0

    lax.fori_loop(0, FF // 256, widen, 0)
    for t in range(4):
        cols = slice(t * 256, (t + 1) * 256)
        down_part = jnp.dot(hid[...], wd[:, cols], preferred_element_type=F32)
        mixed_ref[:, cols] = (resid[:, cols] + down_part).astype(BF16)

    def kv_end(o, _):
        kv_arrival(o).wait_recv()
        kv_copy(o).wait_send()
        return 0

    lax.fori_loop(1, 16, kv_end, 0)
    kv_own.wait()
    for i in range(4):
        y_copy(head, i, own_sem.at[0, i], 1, up).wait_send()
        y_copy(head, i, own_sem.at[1, i], 2, down).wait_send()
        y_copy(head, i, fwd_sem.at[i], 3, up).wait_send()
        for kind in range(4):
            twin_copy(head, i, kind).wait_send()
    for i in (0, 1, 2, 5, 6, 7):
        remote(wmine, wmine, ws_sem.at[i], wy_sem.at[1], seq, up).wait_send()
    half = wo.at[head, pl.ds(0, 64)]
    for i in (3, 4):
        remote(half, half, ws_sem.at[i], wy_sem.at[1], seq, up).wait_send()
    for i in range(2):
        for kind in range(3):
            g_copy(0, i, gs_sem.at[kind, i], 1, znext).wait_send()
    remote(srow, sin, hs_sem.at[0], hr_sem.at[0], xnext, head).wait_send()
    remote(ysend, xin, hs_sem.at[1], hr_sem.at[1], xnext, head).wait_send()
    for oy, oc in turns:
        ret_copy(oy, oc).wait_send()


def settle_kernel(rowof_ref, mixed_in, kv_in, mixed_out, kv_out, sem, sems):
    whole = pltpu.make_async_copy(mixed_in, mixed_out, sem)
    whole.start()
    moves = [pltpu.make_async_copy(kv_in.at[i], kv_out.at[rowof_ref[i]], sems.at[i]) for i in range(BPS)]
    for move in moves:
        move.start()
    for move in moves:
        move.wait()
    whole.wait()


def per_device(
    tokens, norm_gain, w_qkv, w_mem_gates, persist_keys, persist_values, alpha_bias, eta_bias,
    w_out, ffn_gain, w_gate, w_up, w_down, segment_ids, block_table,
):
    vmem = pl.BlockSpec(memory_space=pltpu.VMEM)
    smem = pl.BlockSpec(memory_space=pltpu.SMEM)
    anywhere = pl.BlockSpec(memory_space=pl.ANY)
    dma = pltpu.SemaphoreType.DMA
    mixed, arrived, rowof = pl.pallas_call(
        layer_kernel,
        out_shape=(
            jax.ShapeDtypeStruct((ROWS, D), BF16),
            jax.ShapeDtypeStruct((BPS, SPAN, 2 * HD), BF16),
            jax.ShapeDtypeStruct((BPS,), jnp.int32),
        ),
        in_specs=[smem] * 3 + [anywhere] + [vmem] * 9 + [anywhere] * 3,
        out_specs=(vmem, anywhere, smem),
        scratch_shapes=[
            pltpu.SMEM((BPS * SPAN,), jnp.int32),
            pltpu.SMEM((1024,), jnp.int32),
            pltpu.SMEM((BPS,), jnp.int32),
            pltpu.VMEM((8, ROWS, D), BF16),
            pltpu.VMEM((8, HD, D), BF16),
            pltpu.VMEM((D, FF), BF16),
            pltpu.VMEM((D, FF), BF16),
            pltpu.VMEM((FF, D), BF16),
            pltpu.VMEM((BPS, SPAN, 2 * HD), BF16),
            pltpu.VMEM((BPS, SPAN, 2 * HD), BF16),
            pltpu.VMEM((8, ROWS, 2 * HD), BF16),
            pltpu.VMEM((8, ROWS, HD), F32),
            pltpu.VMEM((4, 2 * HD, 3 * HD), F32),
            pltpu.VMEM((4, 2 * HD, 3 * HD), BF16),
            pltpu.VMEM((2 * HD, 3 * HD), BF16),
            pltpu.VMEM((2 * HD, HD), BF16),
            pltpu.VMEM((2 * HD, HD), BF16),
            pltpu.VMEM((2 * HD, HD), BF16),
            pltpu.VMEM((2 * HD, HD), BF16),
            pltpu.VMEM((8, ROWS, HD), BF16),
            pltpu.VMEM((8, ROWS, HD), BF16),
            pltpu.VMEM((ROWS, D), F32),
            pltpu.VMEM((ROWS, D), BF16),
            pltpu.VMEM((ROWS, FF), BF16),
            dma((5,)), dma,
            dma((2, 4)), dma((4,)), dma((4, 4)), dma((4, 4)), dma((4, 4)),
            dma((8,)), dma((4,)), dma((4,)),
            dma((3, 2)), dma((4, 2)),
            dma((2,)), dma((2,)),
            dma((8,)), dma((8,)),
            dma((16,)), dma((16,)),
        ],
        compiler_params=pltpu.CompilerParams(
            collective_id=0, has_side_effects=True, vmem_limit_bytes=56 * MIB
        ),
    )(
        alpha_bias, eta_bias, block_table, segment_ids,
        block_table.reshape(4, 128), tokens, norm_gain.reshape(1, D), w_qkv.reshape(D, 3 * HD), w_mem_gates.reshape(3, HD),
        persist_keys, persist_values, w_out, ffn_gain.reshape(1, D),
        w_gate, w_up, w_down,
    )

    return pl.pallas_call(
        settle_kernel,
        out_shape=(
            jax.ShapeDtypeStruct((ROWS, D), BF16),
            jax.ShapeDtypeStruct((BPS, SPAN, 2 * HD), BF16),
        ),
        in_specs=[smem, anywhere, anywhere],
        out_specs=(anywhere, anywhere),
        scratch_shapes=[dma, dma((BPS,))],
    )(rowof, mixed, arrived)


def solution(mesh):
    return jax.shard_map(
        per_device,
        mesh=mesh,
        in_specs=(
            P(("seq", "head"), None),
            P(),
            P(None, "head", None),
            P("head", None, None),
            P(None, "head"),
            P(None, "head"),
            P("head"),
            P("head"),
            P("head", None),
            P(),
            P(),
            P(),
            P(),
            P(),
            P(),
        ),
        out_specs=(P(("seq", "head"), None), P("seq", None, "head")),
        check_vma=False,
    )
```

```python
import jax
import jax.numpy as jnp
from jax import lax
from jax.experimental import pallas as pl
from jax.experimental.pallas import tpu as pltpu
from jax.sharding import PartitionSpec as P

D = 1024
HD = 128
FF = 2816
PERS = 16
SPAN = 64
ROWS = 256
PIECE = 64
TOKENS = 32768
BPS = 32
EPS = 1e-05
TINY = 1e-06
MIB = 1 << 20
MESH = pl.DeviceIdType.MESH
F32 = jnp.float32
BF16 = jnp.bfloat16


def sigmoid(x):
    return 1.0 / (1.0 + jnp.exp(-x))


def unit(x):
    return x * lax.rsqrt(jnp.mean(x * x, axis=-1, keepdims=True) + TINY)


def mm(a, b):
    return jnp.dot(a.astype(BF16), b.astype(BF16), preferred_element_type=F32)


def compose(later, earlier):
    joined = mm(later[:, :256], earlier)
    return joined[:, :256], joined[:, 256:] + later[:, 256:]


def layer_kernel(
    ab_ref, eb_ref, table_ref, ids_hbm,
    wide_table_ref, tokens_ref, ngain_ref, wq_ref, wmg_ref, pk_ref, pv_ref, wout_ref, fgain_ref,
    wg_hbm, wu_hbm, wd_hbm,
    mixed_ref, kv_hbm, rowof_ref,
    ids, before, order, xg, wo, wg, wu, wd, kvbuf, kvsend, rm, rs, pt, gmap, pz, srow, sin, ysend, xin,
    retsend, ret, resid, ffn_in, hid,
    local_sem, kvl_sem, own_sem, fwd_sem, tws_sem, yr_sem, twr_sem, ws_sem, wy_sem, wc_sem,
    gs_sem, gr_sem, hs_sem, hr_sem, as_sem, ar_sem, ks_sem, kr_sem,
):
    seq = lax.axis_index("seq")
    head = lax.axis_index("head")
    sx, sz = seq // 4, seq % 4
    y, c = head // 2, head % 2
    up = ((y + 1) % 4) * 2 + c
    down = ((y + 3) % 4) * 2 + c
    twin = y * 2 + (1 - c)
    znext = sx * 4 + (sz + 1) % 4
    zprev = sx * 4 + (sz + 3) % 4
    xnext = ((sx + 1) % 4) * 4 + sz

    def remote(src, dst, ssem, rsem, s, h):
        return pltpu.make_async_remote_copy(
            src_ref=src, dst_ref=dst, send_sem=ssem, recv_sem=rsem, device_id=(s, h), device_id_type=MESH
        )

    loads = [
        pltpu.make_async_copy(wg_hbm, wg, local_sem.at[0]),
        pltpu.make_async_copy(wu_hbm, wu, local_sem.at[1]),
        pltpu.make_async_copy(wd_hbm, wd, local_sem.at[2]),
    ]
    mine_ids = pl.multiple_of(seq * (BPS * SPAN), 1024)
    prior_ids = pl.multiple_of((seq * (BPS * SPAN) + TOKENS - 1024) % TOKENS, 1024)
    id_loads = [
        pltpu.make_async_copy(ids_hbm.at[pl.ds(mine_ids, BPS * SPAN)], ids, local_sem.at[3]),
        pltpu.make_async_copy(ids_hbm.at[pl.ds(prior_ids, 1024)], before, local_sem.at[4]),
    ]
    for load in id_loads:
        load.start()

    barrier = pltpu.get_barrier_semaphore()

    def greet_head(o, _):
        pl.semaphore_signal(barrier, inc=1, device_id=(seq, (head + o) % 8), device_id_type=MESH)
        return 0

    def greet_seq(o, _):
        pl.semaphore_signal(barrier, inc=1, device_id=((seq + o) % 16, head), device_id_type=MESH)
        return 0

    lax.fori_loop(1, 8, greet_head, 0)
    lax.fori_loop(1, 16, greet_seq, 0)

    tok = tokens_ref[...].astype(F32)
    scale = lax.rsqrt(jnp.mean(tok * tok, axis=-1, keepdims=True) + EPS)
    xg[head] = (tok * scale * ngain_ref[...]).astype(BF16)

    pl.semaphore_wait(barrier, 22)

    def piece(slot, i):
        return xg.at[slot, pl.ds(i * PIECE, PIECE)]

    def y_copy(slot, i, sem, kind, to):
        part = piece(slot, i)
        return remote(part, part, sem, yr_sem.at[kind, i], seq, to)

    def twin_copy(slot, i, kind):
        part = piece(slot, i)
        return remote(part, part, tws_sem.at[kind, i], twr_sem.at[kind, i], seq, twin)

    slots = [2 * ((y + off) % 4) + c for off in (0, 3, 1, 2)]
    others = [2 * ((y + off) % 4) + 1 - c for off in (0, 3, 1, 2)]
    for i in range(4):
        y_copy(head, i, own_sem.at[0, i], 1, up).start()
        y_copy(head, 3 - i, own_sem.at[1, 3 - i], 2, down).start()
    for i in range(4):
        twin_copy(head, i, 0).start()
    for load in loads:
        load.start()

    initial = jnp.dot(
        pk_ref[...].astype(F32).T.astype(BF16), pv_ref[...], preferred_element_type=F32
    ) * (1.0 / PERS)
    row = lax.broadcasted_iota(jnp.int32, (HD, 3 * HD), 0)
    col = lax.broadcasted_iota(jnp.int32, (HD, 3 * HD), 1)
    eye_m = (row == col).astype(F32)
    eye_s = (row + HD == col).astype(F32)
    zero_wide = jnp.zeros((HD, 2 * HD), F32)
    fresh = jnp.concatenate([zero_wide, initial], axis=1)
    zero_rows = jnp.zeros((SPAN, 2 * HD), F32)

    wide = wide_table_ref[...]
    place_no = lax.broadcasted_iota(jnp.int32, (4, 128), 0) * 128 + lax.broadcasted_iota(jnp.int32, (4, 128), 1)
    owner_no = lax.shift_right_logical(wide, 5)
    key_no = owner_no * BPS + (place_no & (BPS - 1))
    position = jnp.zeros((4, 128), jnp.int32)
    for i in range(BPS):
        one = lax.shift_right_logical(table_ref[seq * BPS + i], 5) * BPS + i
        position = position + (one < key_no).astype(jnp.int32)
    position = jnp.where(lax.shift_right_logical(place_no, 5) == seq, position, -1)
    owned = (owner_no == seq).astype(F32)
    earlier = lax.broadcasted_iota(jnp.int32, (128, 128), 0) < lax.broadcasted_iota(jnp.int32, (128, 128), 1)
    rank = mm(jnp.concatenate([owned, owned], axis=0), earlier.astype(F32))[:4]
    rank = rank + 8.0 * lax.broadcasted_iota(jnp.int32, (4, 128), 0).astype(F32)
    rank = jnp.where(owned > 0.0, rank, -1.0)
    for i in range(BPS):
        order[i] = jnp.sum(jnp.where(position == i, place_no & (BPS - 1), 0))
        rowof_ref[i] = jnp.sum(jnp.where(rank == float(i), wide & (BPS - 1), 0))
    for load in id_loads:
        load.wait()

    def keep_of(yp, b):
        block = yp * 8 + b
        here = ids[block * SPAN]
        there = ids[jnp.maximum(block * SPAN - 1, 0)]
        there = jnp.where(block == 0, before[1023], there)
        there = jnp.where(block + seq == 0, -1, there)
        return jnp.where(here == there, 1.0, 0.0)

    def process(chips):
        work = []
        for yp in chips:
            x = xg[pl.ds(2 * yp, 2)].reshape(2 * ROWS, D)
            proj = jnp.dot(x, wq_ref[...], preferred_element_type=F32)
            q = unit(proj[:, :HD]) * HD ** (-0.5)
            k = unit(proj[:, HD : 2 * HD]) * HD ** (-0.5)
            v = proj[:, 2 * HD :]
            wmg = wmg_ref[...].astype(F32)
            theta = sigmoid(jnp.sum(v * wmg[0:1], axis=-1, keepdims=True)) * (1.0 / SPAN)
            mean_v = jnp.mean(v.reshape(8, SPAN, HD), axis=1)
            alpha = sigmoid(jnp.sum(mean_v * wmg[1:2], axis=-1, keepdims=True) + ab_ref[0])
            eta = sigmoid(jnp.sum(mean_v * wmg[2:3], axis=-1, keepdims=True) + eb_ref[0])
            qb, kb = q.astype(BF16), k.astype(BF16)
            kvbuf[pl.ds(yp * 8, 8), :, :HD] = kb.reshape(8, SPAN, HD)
            kvbuf[pl.ds(yp * 8, 8), :, HD:] = v.astype(BF16).reshape(8, SPAN, HD)
            for half in range(2):
                work.append([yp, half * 4, qb, k, kb, v, theta, alpha, eta, eye_m, eye_s, []])
        for step in range(4):
            for item in work:
                yp, first_block, qb, k, kb, v, theta, alpha, eta, memory, moment, reads = item
                b = first_block + step
                rows = slice(b * SPAN, (b + 1) * SPAN)
                keep = keep_of(yp, b)
                held = keep * memory + (1.0 - keep) * fresh
                both = mm(jnp.concatenate([qb[rows], kb[rows]], axis=0), held)
                reads.append(both[:SPAN])
                wide_v = jnp.concatenate([zero_rows, v[rows]], axis=1)
                push = theta[rows] * (wide_v - both[SPAN:])
                moment = eta[b : b + 1] * (keep * moment) + mm(k[rows].T, push)
                memory = (1.0 - alpha[b : b + 1]) * held + moment
                item[9], item[10] = memory, moment
        for i in range(0, len(work), 2):
            yp = work[i][0]
            even = jnp.concatenate([work[i][9], work[i][10]], axis=0)
            odd = jnp.concatenate([work[i + 1][9], work[i + 1][10]], axis=0)
            tmap, tshift = compose(odd, even)
            pt[yp, :, :256] = tmap
            pt[yp, :, 256:] = tshift
            read_even = jnp.concatenate(work[i][11], axis=0)
            read_odd = jnp.concatenate(work[i + 1][11], axis=0)
            omap, oshift = compose(read_odd, even)
            rm[2 * yp] = read_even[:, :256].astype(BF16)
            rs[2 * yp] = read_even[:, 256:]
            rm[2 * yp + 1] = omap.astype(BF16)
            rs[2 * yp + 1] = oshift

    def twin_in(kind):
        for i in range(4):
            twin_copy(others[kind], i, kind).wait_recv()

    twin_in(0)
    process([y])
    for i in range(4):
        y_copy(slots[1], i, own_sem.at[0, 0], 1, up).wait_recv()
        if i < 2:
            y_copy(slots[1], i, fwd_sem.at[i], 3, up).start()
        twin_copy(slots[1], i, 1).start()
        y_copy(slots[2], 3 - i, own_sem.at[0, 0], 2, up).wait_recv()
        if i < 2:
            y_copy(slots[2], 3 - i, fwd_sem.at[3 - i], 3, down).start()
        twin_copy(slots[2], 3 - i, 2).start()
    twin_in(1)
    twin_in(2)
    process([(y + 3) % 4, (y + 1) % 4])
    for i in (0, 3, 1, 2):
        y_copy(slots[3], i, own_sem.at[0, 0], 3, up).wait_recv()
        twin_copy(slots[3], i, 3).start()
    twin_in(3)
    process([(y + 2) % 4])

    def join(later, earlier):
        return jnp.concatenate(compose(later, earlier), axis=1)

    first = join(pt[1], pt[0])
    total = join(join(pt[3], pt[2]), first)
    gmap[sz] = total.astype(BF16)
    def g_copy(step, i, sem, kind, to):
        part = gmap.at[(sz + step) % 4, pl.ds(i * HD, HD)]
        return remote(part, part, sem, gr_sem.at[kind, i], to, head)

    for i in range(2):
        g_copy(0, i, gs_sem.at[0, i], 1, znext).start()
        g_copy(0, 1 - i, gs_sem.at[1, 1 - i], 2, zprev).start()

    wo[head] = wout_ref[...]
    wmine = wo.at[head]
    remote(wmine, wmine, ws_sem.at[1], wy_sem.at[1], seq, up).start()
    remote(wmine, wmine, ws_sem.at[2], wy_sem.at[2], seq, down).start()
    remote(wmine, wmine, ws_sem.at[0], wc_sem.at[0], seq, twin).start()

    def fold(p, emap):
        read = rm[pl.ds(2 * p, 2)].reshape(2 * ROWS, 2 * HD)
        out = jnp.dot(read, emap.astype(BF16), preferred_element_type=F32)
        rm[pl.ds(2 * p, 2)] = out[:, :256].astype(BF16).reshape(2, ROWS, 2 * HD)
        rs[pl.ds(2 * p, 2)] = rs[pl.ds(2 * p, 2)] + out[:, 256:].reshape(2, ROWS, HD)

    fold(1, pt[0])
    fold(2, first)
    fold(3, join(pt[2], first))

    def place(p, _):
        kvsend[p] = kvbuf[order[p]]
        return 0

    lax.fori_loop(0, BPS, place, 0)

    g_copy(3, 0, gs_sem.at[0, 0], 1, znext).wait_recv()
    g_copy(3, 0, gs_sem.at[2, 0], 3, znext).start()
    g_copy(1, 1, gs_sem.at[0, 0], 2, znext).wait_recv()
    g_copy(1, 1, gs_sem.at[2, 1], 3, zprev).start()
    g_copy(3, 1, gs_sem.at[0, 0], 1, znext).wait_recv()
    g_copy(1, 0, gs_sem.at[0, 0], 2, znext).wait_recv()
    g_copy(2, 0, gs_sem.at[0, 0], 3, znext).wait_recv()
    g_copy(2, 1, gs_sem.at[0, 0], 3, znext).wait_recv()

    def bjoin(later, earlier):
        tmap, tshift = compose(later.astype(F32), earlier)
        return jnp.concatenate([tmap, tshift], axis=1)

    low = bjoin(gmap[1], gmap[0])
    total = join(bjoin(gmap[3], gmap[2]), low)
    srow[...] = total[:, 256:].astype(BF16)
    remote(srow, sin, hs_sem.at[0], hr_sem.at[0], xnext, head).start()

    @pl.when(sz == 1)
    def _():
        pz[...] = gmap[0]

    @pl.when(sz == 2)
    def _():
        pz[...] = low.astype(BF16)

    @pl.when(sz == 3)
    def _():
        pz[...] = bjoin(gmap[2], low).astype(BF16)

    wprev, wnext = wo.at[((y + 3) % 4) * 2 + c], wo.at[((y + 1) % 4) * 2 + c]
    remote(wprev, wprev, ws_sem.at[1], wy_sem.at[1], seq, up).wait_recv()
    half = wo.at[((y + 3) % 4) * 2 + c, pl.ds(0, 64)]
    remote(half, half, ws_sem.at[3], wy_sem.at[3], seq, up).start()
    remote(wprev, wprev, ws_sem.at[5], wc_sem.at[1], seq, twin).start()
    remote(wnext, wnext, ws_sem.at[1], wy_sem.at[2], seq, up).wait_recv()
    half = wo.at[((y + 1) % 4) * 2 + c, pl.ds(64, 64)]
    remote(half, half, ws_sem.at[4], wy_sem.at[3], seq, down).start()
    remote(wnext, wnext, ws_sem.at[6], wc_sem.at[2], seq, twin).start()

    remote(srow, sin, hs_sem.at[0], hr_sem.at[0], xnext, head).wait_recv()
    ysend[...] = (mm(total[:, :256], sin[...]) + total[:, 256:]).astype(BF16)
    remote(ysend, xin, hs_sem.at[1], hr_sem.at[1], xnext, head).start()

    @pl.when(sz > 0)
    def _():
        def fold_all(p, _):
            fold(p, pz[...])
            return 0

        lax.fori_loop(0, 4, fold_all, 0)

    def kv_copy(o):
        to = (seq + o) % 16
        return remote(
            kvsend.at[pl.ds(2 * to, 2)], kv_hbm.at[pl.ds(2 * seq, 2)], ks_sem.at[o], kr_sem.at[o], to, head
        )

    def kv_arrival(o):
        source = (seq + 16 - o) % 16
        return remote(
            kvsend.at[pl.ds(2 * source, 2)], kv_hbm.at[pl.ds(2 * source, 2)], ks_sem.at[o], kr_sem.at[o], source, head
        )

    def kv_start(o, _):
        kv_copy(o).start()
        return 0

    lax.fori_loop(1, 16, kv_start, 0)
    kv_own = pltpu.make_async_copy(kvsend.at[pl.ds(2 * seq, 2)], kv_hbm.at[pl.ds(2 * seq, 2)], kvl_sem)
    kv_own.start()

    wfar = wo.at[((y + 2) % 4) * 2 + c]
    remote(wfar, wfar, ws_sem.at[1], wy_sem.at[3], seq, up).wait_recv()
    remote(wfar, wfar, ws_sem.at[7], wc_sem.at[3], seq, twin).start()

    remote(ysend, xin, hs_sem.at[1], hr_sem.at[1], xnext, head).wait_recv()
    enter = xin[...]

    def answer(j):
        recalled = jnp.dot(rm[j], enter, preferred_element_type=F32) + rs[j]
        return unit(recalled).astype(BF16)

    def ret_copy(oy, oc):
        o = oy * 2 + oc
        to = ((y + oy) % 4) * 2 + (c + oc) % 2
        return remote(retsend.at[o], ret.at[head], as_sem.at[o], ar_sem.at[o], seq, to)

    def ret_arrival(oy, oc):
        o = oy * 2 + oc
        source = ((y + 4 - oy) % 4) * 2 + (c + oc) % 2
        return remote(retsend.at[o], ret.at[source], as_sem.at[o], ar_sem.at[o], seq, source)

    turns = [(2, 0), (2, 1), (1, 0), (1, 1), (3, 0), (3, 1), (0, 1)]
    for oy, oc in turns:
        retsend[oy * 2 + oc] = answer(((y + oy) % 4) * 2 + (c + oc) % 2)
        ret_copy(oy, oc).start()
    ret[head] = answer(head)

    for p, off in ((0, 0), (1, 3), (2, 1), (3, 2)):
        other = wo.at[((y + off) % 4) * 2 + 1 - c]
        remote(other, other, ws_sem.at[0], wc_sem.at[p], seq, twin).wait_recv()
    for load in loads:
        load.wait()
    for oy, oc in turns:
        ret_arrival(oy, oc).wait_recv()

    total = tokens_ref[...].astype(F32)
    for i in range(4):
        left = jnp.concatenate([ret[2 * i], ret[2 * i + 1]], axis=1)
        total = total + jnp.dot(left, wo[2 * i : 2 * i + 2].reshape(2 * HD, D), preferred_element_type=F32)
    resid[...] = total
    scale = lax.rsqrt(jnp.mean(total * total, axis=-1, keepdims=True) + EPS)
    ffn_in[...] = (total * scale * fgain_ref[...]).astype(BF16)

    def widen(t, _):
        cols = pl.ds(pl.multiple_of(t * 256, 256), 256)
        gate = jnp.dot(ffn_in[...], wg[:, cols], preferred_element_type=F32)
        upper = jnp.dot(ffn_in[...], wu[:, cols], preferred_element_type=F32)
        hid[:, cols] = (gate / (1.0 + jnp.exp(-gate)) * upper).astype(BF16)
        return 0

    lax.fori_loop(0, FF // 256, widen, 0)
    for t in range(4):
        cols = slice(t * 256, (t + 1) * 256)
        down_part = jnp.dot(hid[...], wd[:, cols], preferred_element_type=F32)
        mixed_ref[:, cols] = (resid[:, cols] + down_part).astype(BF16)

    def kv_end(o, _):
        kv_arrival(o).wait_recv()
        kv_copy(o).wait_send()
        return 0

    lax.fori_loop(1, 16, kv_end, 0)
    kv_own.wait()
    for i in range(4):
        y_copy(head, i, own_sem.at[0, i], 1, up).wait_send()
        y_copy(head, i, own_sem.at[1, i], 2, down).wait_send()
        y_copy(head, i, fwd_sem.at[i], 3, up).wait_send()
        for kind in range(4):
            twin_copy(head, i, kind).wait_send()
    for i in (0, 1, 2, 5, 6, 7):
        remote(wmine, wmine, ws_sem.at[i], wy_sem.at[1], seq, up).wait_send()
    half = wo.at[head, pl.ds(0, 64)]
    for i in (3, 4):
        remote(half, half, ws_sem.at[i], wy_sem.at[1], seq, up).wait_send()
    for i in range(2):
        for kind in range(3):
            g_copy(0, i, gs_sem.at[kind, i], 1, znext).wait_send()
    remote(srow, sin, hs_sem.at[0], hr_sem.at[0], xnext, head).wait_send()
    remote(ysend, xin, hs_sem.at[1], hr_sem.at[1], xnext, head).wait_send()
    for oy, oc in turns:
        ret_copy(oy, oc).wait_send()


def settle_kernel(rowof_ref, mixed_in, kv_in, mixed_out, kv_out, mixed_at, kv_at, in_sem, out_sem, kv_sem):
    halves = [pl.ds(i * 128, 128) for i in range(2)]
    groups = [pl.ds(i * 4, 4) for i in range(8)]
    loads = [pltpu.make_async_copy(kv_in.at[g], kv_at.at[g], in_sem.at[i]) for i, g in enumerate(groups)]
    loads += [pltpu.make_async_copy(mixed_in.at[h], mixed_at.at[h], in_sem.at[8 + i]) for i, h in enumerate(halves)]
    for load in loads:
        load.start()
    stores = [pltpu.make_async_copy(kv_at.at[i], kv_out.at[rowof_ref[i]], kv_sem.at[i]) for i in range(BPS)]
    whole = [pltpu.make_async_copy(mixed_at.at[h], mixed_out.at[h], out_sem.at[i]) for i, h in enumerate(halves)]
    for i in range(8):
        loads[i].wait()
        for b in range(4):
            stores[4 * i + b].start()
    for i in range(2):
        loads[8 + i].wait()
        whole[i].start()
    for store in stores + whole:
        store.wait()


def per_device(
    tokens, norm_gain, w_qkv, w_mem_gates, persist_keys, persist_values, alpha_bias, eta_bias,
    w_out, ffn_gain, w_gate, w_up, w_down, segment_ids, block_table,
):
    vmem = pl.BlockSpec(memory_space=pltpu.VMEM)
    smem = pl.BlockSpec(memory_space=pltpu.SMEM)
    anywhere = pl.BlockSpec(memory_space=pl.ANY)
    dma = pltpu.SemaphoreType.DMA
    mixed, arrived, rowof = pl.pallas_call(
        layer_kernel,
        out_shape=(
            jax.ShapeDtypeStruct((ROWS, D), BF16),
            jax.ShapeDtypeStruct((BPS, SPAN, 2 * HD), BF16),
            jax.ShapeDtypeStruct((BPS,), jnp.int32),
        ),
        in_specs=[smem] * 3 + [anywhere] + [vmem] * 9 + [anywhere] * 3,
        out_specs=(vmem, anywhere, smem),
        scratch_shapes=[
            pltpu.SMEM((BPS * SPAN,), jnp.int32),
            pltpu.SMEM((1024,), jnp.int32),
            pltpu.SMEM((BPS,), jnp.int32),
            pltpu.VMEM((8, ROWS, D), BF16),
            pltpu.VMEM((8, HD, D), BF16),
            pltpu.VMEM((D, FF), BF16),
            pltpu.VMEM((D, FF), BF16),
            pltpu.VMEM((FF, D), BF16),
            pltpu.VMEM((BPS, SPAN, 2 * HD), BF16),
            pltpu.VMEM((BPS, SPAN, 2 * HD), BF16),
            pltpu.VMEM((8, ROWS, 2 * HD), BF16),
            pltpu.VMEM((8, ROWS, HD), F32),
            pltpu.VMEM((4, 2 * HD, 3 * HD), F32),
            pltpu.VMEM((4, 2 * HD, 3 * HD), BF16),
            pltpu.VMEM((2 * HD, 3 * HD), BF16),
            pltpu.VMEM((2 * HD, HD), BF16),
            pltpu.VMEM((2 * HD, HD), BF16),
            pltpu.VMEM((2 * HD, HD), BF16),
            pltpu.VMEM((2 * HD, HD), BF16),
            pltpu.VMEM((8, ROWS, HD), BF16),
            pltpu.VMEM((8, ROWS, HD), BF16),
            pltpu.VMEM((ROWS, D), F32),
            pltpu.VMEM((ROWS, D), BF16),
            pltpu.VMEM((ROWS, FF), BF16),
            dma((5,)), dma,
            dma((2, 4)), dma((4,)), dma((4, 4)), dma((4, 4)), dma((4, 4)),
            dma((8,)), dma((4,)), dma((4,)),
            dma((3, 2)), dma((4, 2)),
            dma((2,)), dma((2,)),
            dma((8,)), dma((8,)),
            dma((16,)), dma((16,)),
        ],
        compiler_params=pltpu.CompilerParams(
            collective_id=0, has_side_effects=True, vmem_limit_bytes=56 * MIB
        ),
    )(
        alpha_bias, eta_bias, block_table, segment_ids,
        block_table.reshape(4, 128), tokens, norm_gain.reshape(1, D), w_qkv.reshape(D, 3 * HD), w_mem_gates.reshape(3, HD),
        persist_keys, persist_values, w_out, ffn_gain.reshape(1, D),
        w_gate, w_up, w_down,
    )

    return pl.pallas_call(
        settle_kernel,
        out_shape=(
            jax.ShapeDtypeStruct((ROWS, D), BF16),
            jax.ShapeDtypeStruct((BPS, SPAN, 2 * HD), BF16),
        ),
        in_specs=[smem, anywhere, anywhere],
        out_specs=(anywhere, anywhere),
        scratch_shapes=[
            pltpu.VMEM((ROWS, D), BF16),
            pltpu.VMEM((BPS, SPAN, 2 * HD), BF16),
            dma((10,)), dma((2,)), dma((BPS,)),
        ],
    )(rowof, mixed, arrived)


def solution(mesh):
    return jax.shard_map(
        per_device,
        mesh=mesh,
        in_specs=(
            P(("seq", "head"), None),
            P(),
            P(None, "head", None),
            P("head", None, None),
            P(None, "head"),
            P(None, "head"),
            P("head"),
            P("head"),
            P("head", None),
            P(),
            P(),
            P(),
            P(),
            P(),
            P(),
        ),
        out_specs=(P(("seq", "head"), None), P("seq", None, "head")),
        check_vma=False,
    )
```

```python
import jax
import jax.numpy as jnp
from jax import lax
from jax.experimental import pallas as pl
from jax.experimental.pallas import tpu as pltpu
from jax.sharding import PartitionSpec as P

D = 1024
HD = 128
FF = 2816
PERS = 16
SPAN = 64
ROWS = 256
PIECE = 64
TOKENS = 32768
BPS = 32
EPS = 1e-05
TINY = 1e-06
MIB = 1 << 20
MESH = pl.DeviceIdType.MESH
F32 = jnp.float32
BF16 = jnp.bfloat16


def sigmoid(x):
    return 1.0 / (1.0 + jnp.exp(-x))


def unit(x):
    return x * lax.rsqrt(jnp.mean(x * x, axis=-1, keepdims=True) + TINY)


def mm(a, b):
    return jnp.dot(a.astype(BF16), b.astype(BF16), preferred_element_type=F32)


def compose(later, earlier):
    joined = mm(later[:, :256], earlier)
    return joined[:, :256], joined[:, 256:] + later[:, 256:]


def layer_kernel(
    ab_ref, eb_ref, table_ref, ids_hbm,
    wide_table_ref, tokens_ref, ngain_ref, wmg_ref, pk_ref, pv_ref, fgain_ref,
    wq_hbm, wout_hbm, wg_hbm, wu_hbm, wd_hbm,
    mixed_ref, kv_hbm, rowof_ref,
    ids, before, order, wq_ref, xg, wo, wg, wu, wd, kvbuf, kvsend, rm, rs, pt, gmap, pz, srow, sin, ysend, xin,
    retsend, ret, resid, ffn_in, hid,
    local_sem, kvl_sem, own_sem, fwd_sem, tws_sem, yr_sem, twr_sem, ws_sem, wy_sem, wc_sem,
    gs_sem, gr_sem, hs_sem, hr_sem, as_sem, ar_sem, ks_sem, kr_sem,
):
    seq = lax.axis_index("seq")
    head = lax.axis_index("head")
    sx, sz = seq // 4, seq % 4
    y, c = head // 2, head % 2
    up = ((y + 1) % 4) * 2 + c
    down = ((y + 3) % 4) * 2 + c
    twin = y * 2 + (1 - c)
    znext = sx * 4 + (sz + 1) % 4
    zprev = sx * 4 + (sz + 3) % 4
    xnext = ((sx + 1) % 4) * 4 + sz

    def remote(src, dst, ssem, rsem, s, h):
        return pltpu.make_async_remote_copy(
            src_ref=src, dst_ref=dst, send_sem=ssem, recv_sem=rsem, device_id=(s, h), device_id_type=MESH
        )

    loads = [
        pltpu.make_async_copy(wg_hbm, wg, local_sem.at[0]),
        pltpu.make_async_copy(wu_hbm, wu, local_sem.at[1]),
        pltpu.make_async_copy(wd_hbm, wd, local_sem.at[2]),
    ]
    mine_ids = pl.multiple_of(seq * (BPS * SPAN), 1024)
    prior_ids = pl.multiple_of((seq * (BPS * SPAN) + TOKENS - 1024) % TOKENS, 1024)
    id_loads = [
        pltpu.make_async_copy(ids_hbm.at[pl.ds(mine_ids, BPS * SPAN)], ids, local_sem.at[3]),
        pltpu.make_async_copy(ids_hbm.at[pl.ds(prior_ids, 1024)], before, local_sem.at[4]),
    ]
    wq_load = pltpu.make_async_copy(wq_hbm, wq_ref, local_sem.at[5])
    wout_load = pltpu.make_async_copy(wout_hbm, wo.at[head], local_sem.at[6])
    for load in id_loads + [wq_load, wout_load]:
        load.start()

    barrier = pltpu.get_barrier_semaphore()

    def greet_head(o, _):
        pl.semaphore_signal(barrier, inc=1, device_id=(seq, (head + o) % 8), device_id_type=MESH)
        return 0

    def greet_seq(o, _):
        pl.semaphore_signal(barrier, inc=1, device_id=((seq + o) % 16, head), device_id_type=MESH)
        return 0

    lax.fori_loop(1, 8, greet_head, 0)
    lax.fori_loop(1, 16, greet_seq, 0)

    tok = tokens_ref[...].astype(F32)
    scale = lax.rsqrt(jnp.mean(tok * tok, axis=-1, keepdims=True) + EPS)
    xg[head] = (tok * scale * ngain_ref[...]).astype(BF16)

    pl.semaphore_wait(barrier, 22)

    def piece(slot, i):
        return xg.at[slot, pl.ds(i * PIECE, PIECE)]

    def y_copy(slot, i, sem, kind, to):
        part = piece(slot, i)
        return remote(part, part, sem, yr_sem.at[kind, i], seq, to)

    def twin_copy(slot, i, kind):
        part = piece(slot, i)
        return remote(part, part, tws_sem.at[kind, i], twr_sem.at[kind, i], seq, twin)

    slots = [2 * ((y + off) % 4) + c for off in (0, 3, 1, 2)]
    others = [2 * ((y + off) % 4) + 1 - c for off in (0, 3, 1, 2)]
    for i in range(4):
        y_copy(head, i, own_sem.at[0, i], 1, up).start()
        y_copy(head, 3 - i, own_sem.at[1, 3 - i], 2, down).start()
    for i in range(4):
        twin_copy(head, i, 0).start()
    for load in loads:
        load.start()

    initial = jnp.dot(
        pk_ref[...].astype(F32).T.astype(BF16), pv_ref[...], preferred_element_type=F32
    ) * (1.0 / PERS)
    row = lax.broadcasted_iota(jnp.int32, (HD, 3 * HD), 0)
    col = lax.broadcasted_iota(jnp.int32, (HD, 3 * HD), 1)
    eye_m = (row == col).astype(F32)
    eye_s = (row + HD == col).astype(F32)
    zero_wide = jnp.zeros((HD, 2 * HD), F32)
    fresh = jnp.concatenate([zero_wide, initial], axis=1)
    zero_rows = jnp.zeros((SPAN, 2 * HD), F32)

    wide = wide_table_ref[...]
    place_no = lax.broadcasted_iota(jnp.int32, (4, 128), 0) * 128 + lax.broadcasted_iota(jnp.int32, (4, 128), 1)
    owner_no = lax.shift_right_logical(wide, 5)
    key_no = owner_no * BPS + (place_no & (BPS - 1))
    position = jnp.zeros((4, 128), jnp.int32)
    for i in range(BPS):
        one = lax.shift_right_logical(table_ref[seq * BPS + i], 5) * BPS + i
        position = position + (one < key_no).astype(jnp.int32)
    position = jnp.where(lax.shift_right_logical(place_no, 5) == seq, position, -1)
    owned = (owner_no == seq).astype(F32)
    earlier = lax.broadcasted_iota(jnp.int32, (128, 128), 0) < lax.broadcasted_iota(jnp.int32, (128, 128), 1)
    rank = mm(jnp.concatenate([owned, owned], axis=0), earlier.astype(F32))[:4]
    rank = rank + 8.0 * lax.broadcasted_iota(jnp.int32, (4, 128), 0).astype(F32)
    rank = jnp.where(owned > 0.0, rank, -1.0)
    for i in range(BPS):
        order[i] = jnp.sum(jnp.where(position == i, place_no & (BPS - 1), 0))
        rowof_ref[i] = jnp.sum(jnp.where(rank == float(i), wide & (BPS - 1), 0))
    for load in id_loads:
        load.wait()

    def keep_of(yp, b):
        block = yp * 8 + b
        here = ids[block * SPAN]
        there = ids[jnp.maximum(block * SPAN - 1, 0)]
        there = jnp.where(block == 0, before[1023], there)
        there = jnp.where(block + seq == 0, -1, there)
        return jnp.where(here == there, 1.0, 0.0)

    def join(later, earlier):
        return jnp.concatenate(compose(later, earlier), axis=1)

    def project(x, first_block, yp):
        proj = jnp.dot(x, wq_ref[...], preferred_element_type=F32)
        q = unit(proj[:, :HD]) * HD ** (-0.5)
        k = unit(proj[:, HD : 2 * HD]) * HD ** (-0.5)
        v = proj[:, 2 * HD :]
        blocks = x.shape[0] // SPAN
        wmg = wmg_ref[...].astype(F32)
        theta = sigmoid(jnp.sum(v * wmg[0:1], axis=-1, keepdims=True)) * (1.0 / SPAN)
        mean_v = jnp.mean(v.reshape(blocks, SPAN, HD), axis=1)
        alpha = sigmoid(jnp.sum(mean_v * wmg[1:2], axis=-1, keepdims=True) + ab_ref[0])
        eta = sigmoid(jnp.sum(mean_v * wmg[2:3], axis=-1, keepdims=True) + eb_ref[0])
        qb, kb = q.astype(BF16), k.astype(BF16)
        kvbuf[pl.ds(yp * 8 + first_block, blocks), :, :HD] = kb.reshape(blocks, SPAN, HD)
        kvbuf[pl.ds(yp * 8 + first_block, blocks), :, HD:] = v.astype(BF16).reshape(blocks, SPAN, HD)
        return qb, k, kb, v, theta, alpha, eta

    def chains(work, steps):
        states = [[eye_m, eye_s, []] for _ in work]
        for step in range(steps):
            for (yp, block, at, (qb, k, kb, v, theta, alpha, eta)), state in zip(work, states):
                b = at + step
                rows = slice(b * SPAN, (b + 1) * SPAN)
                memory, moment, reads = state
                keep = keep_of(yp, block + step)
                held = keep * memory + (1.0 - keep) * fresh
                both = mm(jnp.concatenate([qb[rows], kb[rows]], axis=0), held)
                reads.append(both[:SPAN])
                wide_v = jnp.concatenate([zero_rows, v[rows]], axis=1)
                push = theta[rows] * (wide_v - both[SPAN:])
                moment = eta[b : b + 1] * (keep * moment) + mm(k[rows].T, push)
                state[0] = (1.0 - alpha[b : b + 1]) * held + moment
                state[1] = moment
        return [
            (jnp.concatenate(state[:2], axis=0), jnp.concatenate(state[2], axis=0)) for state in states
        ]

    def append(first, second):
        return join(second[0], first[0]), jnp.concatenate([first[1], join(second[1], first[0])], axis=0)

    def settle(yp, even, odd):
        tmap, reads = append(even, odd)
        pt[yp] = tmap
        rm[pl.ds(2 * yp, 2)] = reads[:, :256].astype(BF16).reshape(2, ROWS, 2 * HD)
        rs[pl.ds(2 * yp, 2)] = reads[:, 256:].reshape(2, ROWS, HD)

    def process(chips):
        work = []
        for yp in chips:
            made = project(xg[pl.ds(2 * yp, 2)].reshape(2 * ROWS, D), 0, yp)
            work += [(yp, 0, 0, made), (yp, 4, 4, made)]
        done = chains(work, 4)
        for i, yp in enumerate(chips):
            settle(yp, done[2 * i], done[2 * i + 1])

    def twin_in(kind):
        for i in range(4):
            twin_copy(others[kind], i, kind).wait_recv()

    wq_load.wait()
    wout_load.wait()
    twin_in(0)
    process([y])
    for i in range(4):
        y_copy(slots[1], i, own_sem.at[0, 0], 1, up).wait_recv()
        if i < 2:
            y_copy(slots[1], i, fwd_sem.at[i], 3, up).start()
        twin_copy(slots[1], i, 1).start()
        y_copy(slots[2], 3 - i, own_sem.at[0, 0], 2, up).wait_recv()
        if i < 2:
            y_copy(slots[2], 3 - i, fwd_sem.at[3 - i], 3, down).start()
        twin_copy(slots[2], 3 - i, 2).start()
    twin_in(1)
    twin_in(2)
    process([(y + 3) % 4, (y + 1) % 4])
    for i in (0, 3, 1, 2):
        y_copy(slots[3], i, own_sem.at[0, 0], 3, up).wait_recv()
        twin_copy(slots[3], i, 3).start()
    far = (y + 2) % 4
    here = project(xg[2 * far + c], 4 * c, far)
    twin_in(3)
    there = project(xg[2 * far + 1 - c], 4 * (1 - c), far)
    done = chains(
        [(far, 4 * c, 0, here), (far, 4 * c + 2, 2, here), (far, 4 - 4 * c, 0, there), (far, 6 - 4 * c, 2, there)], 2
    )
    here, there = append(done[0], done[1]), append(done[2], done[3])
    settle(
        far,
        [jnp.where(c == 0, a, b) for a, b in zip(here, there)],
        [jnp.where(c == 0, b, a) for a, b in zip(here, there)],
    )

    first = join(pt[1], pt[0])
    total = join(join(pt[3], pt[2]), first)
    gmap[sz] = total.astype(BF16)
    def g_copy(step, i, sem, kind, to):
        part = gmap.at[(sz + step) % 4, pl.ds(i * HD, HD)]
        return remote(part, part, sem, gr_sem.at[kind, i], to, head)

    for i in range(2):
        g_copy(0, i, gs_sem.at[0, i], 1, znext).start()
        g_copy(0, 1 - i, gs_sem.at[1, 1 - i], 2, zprev).start()

    wmine = wo.at[head]
    remote(wmine, wmine, ws_sem.at[1], wy_sem.at[1], seq, up).start()
    remote(wmine, wmine, ws_sem.at[2], wy_sem.at[2], seq, down).start()
    remote(wmine, wmine, ws_sem.at[0], wc_sem.at[0], seq, twin).start()

    def fold(p, emap):
        read = rm[pl.ds(2 * p, 2)].reshape(2 * ROWS, 2 * HD)
        out = jnp.dot(read, emap.astype(BF16), preferred_element_type=F32)
        rm[pl.ds(2 * p, 2)] = out[:, :256].astype(BF16).reshape(2, ROWS, 2 * HD)
        rs[pl.ds(2 * p, 2)] = rs[pl.ds(2 * p, 2)] + out[:, 256:].reshape(2, ROWS, HD)

    fold(1, pt[0])
    fold(2, first)
    fold(3, join(pt[2], first))

    def place(p, _):
        kvsend[p] = kvbuf[order[p]]
        return 0

    lax.fori_loop(0, BPS, place, 0)

    def kv_copy(o):
        to = ((sx + o // 4) % 4) * 4 + (sz + o % 4) % 4
        return remote(
            kvsend.at[pl.ds(2 * to, 2)], kv_hbm.at[pl.ds(2 * seq, 2)], ks_sem.at[o], kr_sem.at[o], to, head
        )

    def kv_arrival(o):
        source = ((sx + 4 - o // 4) % 4) * 4 + (sz + 4 - o % 4) % 4
        return remote(
            kvsend.at[pl.ds(2 * source, 2)], kv_hbm.at[pl.ds(2 * source, 2)], ks_sem.at[o], kr_sem.at[o], source, head
        )

    kv_own = pltpu.make_async_copy(kvsend.at[pl.ds(2 * seq, 2)], kv_hbm.at[pl.ds(2 * seq, 2)], kvl_sem)
    kv_own.start()
    for o in (4, 8, 12):
        kv_copy(o).start()

    g_copy(3, 0, gs_sem.at[0, 0], 1, znext).wait_recv()
    g_copy(3, 0, gs_sem.at[2, 0], 3, znext).start()
    g_copy(1, 1, gs_sem.at[0, 0], 2, znext).wait_recv()
    g_copy(1, 1, gs_sem.at[2, 1], 3, zprev).start()
    g_copy(3, 1, gs_sem.at[0, 0], 1, znext).wait_recv()
    g_copy(1, 0, gs_sem.at[0, 0], 2, znext).wait_recv()
    g_copy(2, 0, gs_sem.at[0, 0], 3, znext).wait_recv()
    g_copy(2, 1, gs_sem.at[0, 0], 3, znext).wait_recv()

    def bjoin(later, earlier):
        tmap, tshift = compose(later.astype(F32), earlier)
        return jnp.concatenate([tmap, tshift], axis=1)

    low = bjoin(gmap[1], gmap[0])
    total = join(bjoin(gmap[3], gmap[2]), low)
    srow[...] = total[:, 256:].astype(BF16)
    remote(srow, sin, hs_sem.at[0], hr_sem.at[0], xnext, head).start()

    for o in (1, 2, 3):
        kv_copy(o).start()

    @pl.when(sz == 1)
    def _():
        pz[...] = gmap[0]

    @pl.when(sz == 2)
    def _():
        pz[...] = low.astype(BF16)

    @pl.when(sz == 3)
    def _():
        pz[...] = bjoin(gmap[2], low).astype(BF16)

    wprev, wnext = wo.at[((y + 3) % 4) * 2 + c], wo.at[((y + 1) % 4) * 2 + c]
    remote(wprev, wprev, ws_sem.at[1], wy_sem.at[1], seq, up).wait_recv()
    half = wo.at[((y + 3) % 4) * 2 + c, pl.ds(0, 64)]
    remote(half, half, ws_sem.at[3], wy_sem.at[3], seq, up).start()
    remote(wprev, wprev, ws_sem.at[5], wc_sem.at[1], seq, twin).start()
    remote(wnext, wnext, ws_sem.at[1], wy_sem.at[2], seq, up).wait_recv()
    half = wo.at[((y + 1) % 4) * 2 + c, pl.ds(64, 64)]
    remote(half, half, ws_sem.at[4], wy_sem.at[3], seq, down).start()
    remote(wnext, wnext, ws_sem.at[6], wc_sem.at[2], seq, twin).start()

    remote(srow, sin, hs_sem.at[0], hr_sem.at[0], xnext, head).wait_recv()
    ysend[...] = (mm(total[:, :256], sin[...]) + total[:, 256:]).astype(BF16)
    remote(ysend, xin, hs_sem.at[1], hr_sem.at[1], xnext, head).start()

    @pl.when(sz > 0)
    def _():
        def fold_all(p, _):
            fold(p, pz[...])
            return 0

        lax.fori_loop(0, 4, fold_all, 0)

    wfar = wo.at[((y + 2) % 4) * 2 + c]
    remote(wfar, wfar, ws_sem.at[1], wy_sem.at[3], seq, up).wait_recv()
    remote(wfar, wfar, ws_sem.at[7], wc_sem.at[3], seq, twin).start()

    remote(ysend, xin, hs_sem.at[1], hr_sem.at[1], xnext, head).wait_recv()
    enter = xin[...]

    def answer(j):
        recalled = jnp.dot(rm[j], enter, preferred_element_type=F32) + rs[j]
        return unit(recalled).astype(BF16)

    def ret_copy(oy, oc):
        o = oy * 2 + oc
        to = ((y + oy) % 4) * 2 + (c + oc) % 2
        return remote(retsend.at[o], ret.at[head], as_sem.at[o], ar_sem.at[o], seq, to)

    def ret_arrival(oy, oc):
        o = oy * 2 + oc
        source = ((y + 4 - oy) % 4) * 2 + (c + oc) % 2
        return remote(retsend.at[o], ret.at[source], as_sem.at[o], ar_sem.at[o], seq, source)

    turns = [(2, 0), (2, 1), (1, 0), (1, 1), (3, 0), (3, 1), (0, 1)]
    for oy, oc in turns:
        retsend[oy * 2 + oc] = answer(((y + oy) % 4) * 2 + (c + oc) % 2)
        ret_copy(oy, oc).start()
    for o in (10, 5, 6, 7, 9, 11, 13, 14, 15):
        kv_copy(o).start()
    ret[head] = answer(head)

    total = tokens_ref[...].astype(F32)
    for p, off in ((0, 0), (1, 3), (2, 1), (3, 2)):
        yp = (y + off) % 4
        other = wo.at[2 * yp + 1 - c]
        remote(other, other, ws_sem.at[0], wc_sem.at[p], seq, twin).wait_recv()
        if p > 0:
            ret_arrival((4 - off) % 4, 0).wait_recv()
        ret_arrival((4 - off) % 4, 1).wait_recv()
        left = jnp.concatenate([ret[2 * yp], ret[2 * yp + 1]], axis=1)
        total = total + jnp.dot(left, wo[pl.ds(2 * yp, 2)].reshape(2 * HD, D), preferred_element_type=F32)
    for load in loads:
        load.wait()

    resid[...] = total
    scale = lax.rsqrt(jnp.mean(total * total, axis=-1, keepdims=True) + EPS)
    ffn_in[...] = (total * scale * fgain_ref[...]).astype(BF16)

    for t in range(FF // 256):
        cols = slice(t * 256, (t + 1) * 256)
        gate = jnp.dot(ffn_in[...], wg[:, cols], preferred_element_type=F32)
        upper = jnp.dot(ffn_in[...], wu[:, cols], preferred_element_type=F32)
        hid[:, cols] = (gate / (1.0 + jnp.exp(-gate)) * upper).astype(BF16)
    for t in range(4):
        cols = slice(t * 256, (t + 1) * 256)
        down_part = jnp.dot(hid[...], wd[:, cols], preferred_element_type=F32)
        mixed_ref[:, cols] = (resid[:, cols] + down_part).astype(BF16)

    def kv_end(o, _):
        kv_arrival(o).wait_recv()
        kv_copy(o).wait_send()
        return 0

    lax.fori_loop(1, 16, kv_end, 0)
    kv_own.wait()
    for i in range(4):
        y_copy(head, i, own_sem.at[0, i], 1, up).wait_send()
        y_copy(head, i, own_sem.at[1, i], 2, down).wait_send()
        y_copy(head, i, fwd_sem.at[i], 3, up).wait_send()
        for kind in range(4):
            twin_copy(head, i, kind).wait_send()
    for i in (0, 1, 2, 5, 6, 7):
        remote(wmine, wmine, ws_sem.at[i], wy_sem.at[1], seq, up).wait_send()
    half = wo.at[head, pl.ds(0, 64)]
    for i in (3, 4):
        remote(half, half, ws_sem.at[i], wy_sem.at[1], seq, up).wait_send()
    for i in range(2):
        for kind in range(3):
            g_copy(0, i, gs_sem.at[kind, i], 1, znext).wait_send()
    remote(srow, sin, hs_sem.at[0], hr_sem.at[0], xnext, head).wait_send()
    remote(ysend, xin, hs_sem.at[1], hr_sem.at[1], xnext, head).wait_send()
    for oy, oc in turns:
        ret_copy(oy, oc).wait_send()


def settle_kernel(rowof_ref, mixed_in, kv_in, mixed_out, kv_out, mixed_at, kv_at, in_sem, out_sem, kv_sem):
    halves = [pl.ds(i * 128, 128) for i in range(2)]
    groups = [pl.ds(i * 4, 4) for i in range(8)]
    loads = [pltpu.make_async_copy(kv_in.at[g], kv_at.at[g], in_sem.at[i]) for i, g in enumerate(groups)]
    loads += [pltpu.make_async_copy(mixed_in.at[h], mixed_at.at[h], in_sem.at[8 + i]) for i, h in enumerate(halves)]
    for load in loads:
        load.start()
    stores = [pltpu.make_async_copy(kv_at.at[i], kv_out.at[rowof_ref[i]], kv_sem.at[i]) for i in range(BPS)]
    whole = [pltpu.make_async_copy(mixed_at.at[h], mixed_out.at[h], out_sem.at[i]) for i, h in enumerate(halves)]
    for i in range(8):
        loads[i].wait()
        for b in range(4):
            stores[4 * i + b].start()
    for i in range(2):
        loads[8 + i].wait()
        whole[i].start()
    for store in stores + whole:
        store.wait()


def per_device(
    tokens, norm_gain, w_qkv, w_mem_gates, persist_keys, persist_values, alpha_bias, eta_bias,
    w_out, ffn_gain, w_gate, w_up, w_down, segment_ids, block_table,
):
    vmem = pl.BlockSpec(memory_space=pltpu.VMEM)
    smem = pl.BlockSpec(memory_space=pltpu.SMEM)
    anywhere = pl.BlockSpec(memory_space=pl.ANY)
    dma = pltpu.SemaphoreType.DMA
    mixed, arrived, rowof = pl.pallas_call(
        layer_kernel,
        out_shape=(
            jax.ShapeDtypeStruct((ROWS, D), BF16),
            jax.ShapeDtypeStruct((BPS, SPAN, 2 * HD), BF16),
            jax.ShapeDtypeStruct((BPS,), jnp.int32),
        ),
        in_specs=[smem] * 3 + [anywhere] + [vmem] * 7 + [anywhere] * 5,
        out_specs=(vmem, anywhere, smem),
        scratch_shapes=[
            pltpu.SMEM((BPS * SPAN,), jnp.int32),
            pltpu.SMEM((1024,), jnp.int32),
            pltpu.SMEM((BPS,), jnp.int32),
            pltpu.VMEM((D, 3 * HD), BF16),
            pltpu.VMEM((8, ROWS, D), BF16),
            pltpu.VMEM((8, HD, D), BF16),
            pltpu.VMEM((D, FF), BF16),
            pltpu.VMEM((D, FF), BF16),
            pltpu.VMEM((FF, D), BF16),
            pltpu.VMEM((BPS, SPAN, 2 * HD), BF16),
            pltpu.VMEM((BPS, SPAN, 2 * HD), BF16),
            pltpu.VMEM((8, ROWS, 2 * HD), BF16),
            pltpu.VMEM((8, ROWS, HD), F32),
            pltpu.VMEM((4, 2 * HD, 3 * HD), F32),
            pltpu.VMEM((4, 2 * HD, 3 * HD), BF16),
            pltpu.VMEM((2 * HD, 3 * HD), BF16),
            pltpu.VMEM((2 * HD, HD), BF16),
            pltpu.VMEM((2 * HD, HD), BF16),
            pltpu.VMEM((2 * HD, HD), BF16),
            pltpu.VMEM((2 * HD, HD), BF16),
            pltpu.VMEM((8, ROWS, HD), BF16),
            pltpu.VMEM((8, ROWS, HD), BF16),
            pltpu.VMEM((ROWS, D), F32),
            pltpu.VMEM((ROWS, D), BF16),
            pltpu.VMEM((ROWS, FF), BF16),
            dma((7,)), dma,
            dma((2, 4)), dma((4,)), dma((4, 4)), dma((4, 4)), dma((4, 4)),
            dma((8,)), dma((4,)), dma((4,)),
            dma((3, 2)), dma((4, 2)),
            dma((2,)), dma((2,)),
            dma((8,)), dma((8,)),
            dma((16,)), dma((16,)),
        ],
        compiler_params=pltpu.CompilerParams(
            collective_id=0, has_side_effects=True, vmem_limit_bytes=56 * MIB
        ),
    )(
        alpha_bias, eta_bias, block_table, segment_ids,
        block_table.reshape(4, 128), tokens, norm_gain.reshape(1, D), w_mem_gates.reshape(3, HD),
        persist_keys, persist_values, ffn_gain.reshape(1, D),
        w_qkv.reshape(D, 3 * HD), w_out, w_gate, w_up, w_down,
    )

    return pl.pallas_call(
        settle_kernel,
        out_shape=(
            jax.ShapeDtypeStruct((ROWS, D), BF16),
            jax.ShapeDtypeStruct((BPS, SPAN, 2 * HD), BF16),
        ),
        in_specs=[smem, anywhere, anywhere],
        out_specs=(anywhere, anywhere),
        scratch_shapes=[
            pltpu.VMEM((ROWS, D), BF16),
            pltpu.VMEM((BPS, SPAN, 2 * HD), BF16),
            dma((10,)), dma((2,)), dma((BPS,)),
        ],
    )(rowof, mixed, arrived)


def solution(mesh):
    return jax.shard_map(
        per_device,
        mesh=mesh,
        in_specs=(
            P(("seq", "head"), None),
            P(),
            P(None, "head", None),
            P("head", None, None),
            P(None, "head"),
            P(None, "head"),
            P("head"),
            P("head"),
            P("head", None),
            P(),
            P(),
            P(),
            P(),
            P(),
            P(),
        ),
        out_specs=(P(("seq", "head"), None), P("seq", None, "head")),
        check_vma=False,
    )
```

```python
import jax
import jax.numpy as jnp
from jax import lax
from jax.experimental import pallas as pl
from jax.experimental.pallas import tpu as pltpu
from jax.sharding import PartitionSpec as P

D = 1024
HD = 128
FF = 2816
PERS = 16
SPAN = 64
ROWS = 256
PIECE = 64
HALF = 128
TOKENS = 32768
BPS = 32
EPS = 1e-05
TINY = 1e-06
MIB = 1 << 20
MESH = pl.DeviceIdType.MESH
F32 = jnp.float32
BF16 = jnp.bfloat16


def sigmoid(x):
    return 1.0 / (1.0 + jnp.exp(-x))


def unit(x):
    return x * lax.rsqrt(jnp.mean(x * x, axis=-1, keepdims=True) + TINY)


def mm(a, b):
    return jnp.dot(a.astype(BF16), b.astype(BF16), preferred_element_type=F32)


def compose(later, earlier):
    joined = mm(later[:, :256], earlier)
    return joined[:, :256], joined[:, 256:] + later[:, 256:]


def layer_kernel(
    ab_ref, eb_ref, table_ref, ids_hbm,
    wide_table_ref, tokens_ref, ngain_ref, wmg_ref, pk_ref, pv_ref, fgain_ref,
    wq_hbm, wout_hbm, wg_hbm, wu_hbm, wd_hbm,
    mixed_ref, kv_hbm, rowof_ref,
    ids, before, order, wq_ref, xg, wo, wg, wu, wd, kvbuf, kvsend, rm, rs, pt, gmap, pz, srow, sin, ysend, xin,
    retsend, ret, resid, ffn_in, hid,
    local_sem, kvl_sem, own_sem, fwd_sem, tws_sem, yr_sem, twr_sem, ws_sem, wy_sem, wc_sem,
    gs_sem, gr_sem, hs_sem, hr_sem, as_sem, ar_sem, ks_sem, kr_sem,
):
    seq = lax.axis_index("seq")
    head = lax.axis_index("head")
    sx, sz = seq // 4, seq % 4
    y, c = head // 2, head % 2
    up = ((y + 1) % 4) * 2 + c
    down = ((y + 3) % 4) * 2 + c
    twin = y * 2 + (1 - c)
    znext = sx * 4 + (sz + 1) % 4
    zprev = sx * 4 + (sz + 3) % 4
    xnext = ((sx + 1) % 4) * 4 + sz

    def remote(src, dst, ssem, rsem, s, h):
        return pltpu.make_async_remote_copy(
            src_ref=src, dst_ref=dst, send_sem=ssem, recv_sem=rsem, device_id=(s, h), device_id_type=MESH
        )

    loads = [
        pltpu.make_async_copy(wg_hbm, wg, local_sem.at[0]),
        pltpu.make_async_copy(wu_hbm, wu, local_sem.at[1]),
        pltpu.make_async_copy(wd_hbm, wd, local_sem.at[2]),
    ]
    mine_ids = pl.multiple_of(seq * (BPS * SPAN), 1024)
    prior_ids = pl.multiple_of((seq * (BPS * SPAN) + TOKENS - 1024) % TOKENS, 1024)
    id_loads = [
        pltpu.make_async_copy(ids_hbm.at[pl.ds(mine_ids, BPS * SPAN)], ids, local_sem.at[3]),
        pltpu.make_async_copy(ids_hbm.at[pl.ds(prior_ids, 1024)], before, local_sem.at[4]),
    ]
    wq_load = pltpu.make_async_copy(wq_hbm, wq_ref, local_sem.at[5])
    wout_load = pltpu.make_async_copy(wout_hbm, wo.at[head], local_sem.at[6])
    for load in id_loads + [wq_load, wout_load]:
        load.start()

    barrier = pltpu.get_barrier_semaphore()

    def greet_head(o, _):
        pl.semaphore_signal(barrier, inc=1, device_id=(seq, (head + o) % 8), device_id_type=MESH)
        return 0

    def greet_seq(o, _):
        pl.semaphore_signal(barrier, inc=1, device_id=((seq + o) % 16, head), device_id_type=MESH)
        return 0

    lax.fori_loop(1, 8, greet_head, 0)
    lax.fori_loop(1, 16, greet_seq, 0)

    tok = tokens_ref[...].astype(F32)
    scale = lax.rsqrt(jnp.mean(tok * tok, axis=-1, keepdims=True) + EPS)
    xg[head] = (tok * scale * ngain_ref[...]).astype(BF16)

    pl.semaphore_wait(barrier, 22)

    def piece(slot, i):
        return xg.at[slot, pl.ds(i * PIECE, PIECE)]

    def y_copy(slot, i, sem, kind, to):
        part = piece(slot, i)
        return remote(part, part, sem, yr_sem.at[kind, i], seq, to)

    def twin_copy(slot, i, kind):
        part = piece(slot, i)
        return remote(part, part, tws_sem.at[kind, i], twr_sem.at[kind, i], seq, twin)

    slots = [2 * ((y + off) % 4) + c for off in (0, 3, 1, 2)]
    others = [2 * ((y + off) % 4) + 1 - c for off in (0, 3, 1, 2)]
    for i in range(4):
        y_copy(head, i, own_sem.at[0, i], 1, up).start()
        y_copy(head, 3 - i, own_sem.at[1, 3 - i], 2, down).start()
    for i in range(4):
        twin_copy(head, i, 0).start()
    for load in loads:
        load.start()

    initial = jnp.dot(
        pk_ref[...].astype(F32).T.astype(BF16), pv_ref[...], preferred_element_type=F32
    ) * (1.0 / PERS)
    row = lax.broadcasted_iota(jnp.int32, (HD, 3 * HD), 0)
    col = lax.broadcasted_iota(jnp.int32, (HD, 3 * HD), 1)
    eye_m = (row == col).astype(F32)
    eye_s = (row + HD == col).astype(F32)
    zero_wide = jnp.zeros((HD, 2 * HD), F32)
    fresh = jnp.concatenate([zero_wide, initial], axis=1)
    zero_rows = jnp.zeros((SPAN, 2 * HD), F32)

    wide = wide_table_ref[...]
    place_no = lax.broadcasted_iota(jnp.int32, (4, 128), 0) * 128 + lax.broadcasted_iota(jnp.int32, (4, 128), 1)
    owner_no = lax.shift_right_logical(wide, 5)
    key_no = owner_no * BPS + (place_no & (BPS - 1))
    position = jnp.zeros((4, 128), jnp.int32)
    for i in range(BPS):
        one = lax.shift_right_logical(table_ref[seq * BPS + i], 5) * BPS + i
        position = position + (one < key_no).astype(jnp.int32)
    position = jnp.where(lax.shift_right_logical(place_no, 5) == seq, position, -1)
    owned = (owner_no == seq).astype(F32)
    earlier = lax.broadcasted_iota(jnp.int32, (128, 128), 0) < lax.broadcasted_iota(jnp.int32, (128, 128), 1)
    rank = mm(jnp.concatenate([owned, owned], axis=0), earlier.astype(F32))[:4]
    rank = rank + 8.0 * lax.broadcasted_iota(jnp.int32, (4, 128), 0).astype(F32)
    rank = jnp.where(owned > 0.0, rank, -1.0)
    for i in range(BPS):
        order[i] = jnp.sum(jnp.where(position == i, place_no & (BPS - 1), 0))
        rowof_ref[i] = jnp.sum(jnp.where(rank == float(i), wide & (BPS - 1), 0))
    for load in id_loads:
        load.wait()

    def keep_of(yp, b):
        block = yp * 8 + b
        here = ids[block * SPAN]
        there = ids[jnp.maximum(block * SPAN - 1, 0)]
        there = jnp.where(block == 0, before[1023], there)
        there = jnp.where(block + seq == 0, -1, there)
        return jnp.where(here == there, 1.0, 0.0)

    def join(later, earlier):
        return jnp.concatenate(compose(later, earlier), axis=1)

    def project(x, first_block, yp):
        proj = jnp.dot(x, wq_ref[...], preferred_element_type=F32)
        q = unit(proj[:, :HD]) * HD ** (-0.5)
        k = unit(proj[:, HD : 2 * HD]) * HD ** (-0.5)
        v = proj[:, 2 * HD :]
        blocks = x.shape[0] // SPAN
        wmg = wmg_ref[...].astype(F32)
        theta = sigmoid(jnp.sum(v * wmg[0:1], axis=-1, keepdims=True)) * (1.0 / SPAN)
        mean_v = jnp.mean(v.reshape(blocks, SPAN, HD), axis=1)
        alpha = sigmoid(jnp.sum(mean_v * wmg[1:2], axis=-1, keepdims=True) + ab_ref[0])
        eta = sigmoid(jnp.sum(mean_v * wmg[2:3], axis=-1, keepdims=True) + eb_ref[0])
        qb, kb = q.astype(BF16), k.astype(BF16)
        kvbuf[pl.ds(yp * 8 + first_block, blocks), :, :HD] = kb.reshape(blocks, SPAN, HD)
        kvbuf[pl.ds(yp * 8 + first_block, blocks), :, HD:] = v.astype(BF16).reshape(blocks, SPAN, HD)
        return qb, k, kb, v, theta, alpha, eta

    def chains(work, steps):
        states = [[eye_m, eye_s, []] for _ in work]
        for step in range(steps):
            for (yp, block, at, (qb, k, kb, v, theta, alpha, eta)), state in zip(work, states):
                b = at + step
                rows = slice(b * SPAN, (b + 1) * SPAN)
                memory, moment, reads = state
                keep = keep_of(yp, block + step)
                held = keep * memory + (1.0 - keep) * fresh
                both = mm(jnp.concatenate([qb[rows], kb[rows]], axis=0), held)
                reads.append(both[:SPAN])
                wide_v = jnp.concatenate([zero_rows, v[rows]], axis=1)
                push = theta[rows] * (wide_v - both[SPAN:])
                moment = eta[b : b + 1] * (keep * moment) + mm(k[rows].T, push)
                state[0] = (1.0 - alpha[b : b + 1]) * held + moment
                state[1] = moment
        return [
            (jnp.concatenate(state[:2], axis=0), jnp.concatenate(state[2], axis=0)) for state in states
        ]

    def append(first, second):
        return join(second[0], first[0]), jnp.concatenate([first[1], join(second[1], first[0])], axis=0)

    def settle(yp, even, odd):
        tmap, reads = append(even, odd)
        pt[yp] = tmap
        rm[pl.ds(2 * yp, 2)] = reads[:, :256].astype(BF16).reshape(2, ROWS, 2 * HD)
        rs[pl.ds(2 * yp, 2)] = reads[:, 256:].reshape(2, ROWS, HD)

    def process(chips):
        work = []
        for yp in chips:
            made = project(xg[pl.ds(2 * yp, 2)].reshape(2 * ROWS, D), 0, yp)
            work += [(yp, 0, 0, made), (yp, 4, 4, made)]
        done = chains(work, 4)
        for i, yp in enumerate(chips):
            settle(yp, done[2 * i], done[2 * i + 1])

    def twin_in(kind):
        for i in range(4):
            twin_copy(others[kind], i, kind).wait_recv()

    wq_load.wait()
    wout_load.wait()
    twin_in(0)
    process([y])
    for i in range(4):
        y_copy(slots[1], i, own_sem.at[0, 0], 1, up).wait_recv()
        if i < 2:
            y_copy(slots[1], i, fwd_sem.at[i], 3, up).start()
        twin_copy(slots[1], i, 1).start()
        y_copy(slots[2], 3 - i, own_sem.at[0, 0], 2, up).wait_recv()
        if i < 2:
            y_copy(slots[2], 3 - i, fwd_sem.at[3 - i], 3, down).start()
        twin_copy(slots[2], 3 - i, 2).start()
    twin_in(1)
    twin_in(2)
    process([(y + 3) % 4, (y + 1) % 4])
    for i in (0, 3, 1, 2):
        y_copy(slots[3], i, own_sem.at[0, 0], 3, up).wait_recv()
        twin_copy(slots[3], i, 3).start()
    far = (y + 2) % 4
    here = project(xg[2 * far + c], 4 * c, far)
    twin_in(3)
    there = project(xg[2 * far + 1 - c], 4 * (1 - c), far)
    done = chains(
        [(far, 4 * c, 0, here), (far, 4 * c + 2, 2, here), (far, 4 - 4 * c, 0, there), (far, 6 - 4 * c, 2, there)], 2
    )
    here, there = append(done[0], done[1]), append(done[2], done[3])
    settle(
        far,
        [jnp.where(c == 0, a, b) for a, b in zip(here, there)],
        [jnp.where(c == 0, b, a) for a, b in zip(here, there)],
    )

    first = join(pt[1], pt[0])
    total = join(join(pt[3], pt[2]), first)
    gmap[sz] = total.astype(BF16)
    def g_copy(step, i, sem, kind, to):
        part = gmap.at[(sz + step) % 4, pl.ds(i * HD, HD)]
        return remote(part, part, sem, gr_sem.at[kind, i], to, head)

    for i in range(2):
        g_copy(0, i, gs_sem.at[0, i], 1, znext).start()
        g_copy(0, 1 - i, gs_sem.at[1, 1 - i], 2, zprev).start()

    wmine = wo.at[head]
    remote(wmine, wmine, ws_sem.at[1], wy_sem.at[1], seq, up).start()
    remote(wmine, wmine, ws_sem.at[2], wy_sem.at[2], seq, down).start()
    remote(wmine, wmine, ws_sem.at[0], wc_sem.at[0], seq, twin).start()

    def fold(p, emap):
        read = rm[pl.ds(2 * p, 2)].reshape(2 * ROWS, 2 * HD)
        out = jnp.dot(read, emap.astype(BF16), preferred_element_type=F32)
        rm[pl.ds(2 * p, 2)] = out[:, :256].astype(BF16).reshape(2, ROWS, 2 * HD)
        rs[pl.ds(2 * p, 2)] = rs[pl.ds(2 * p, 2)] + out[:, 256:].reshape(2, ROWS, HD)

    fold(1, pt[0])
    fold(2, first)
    fold(3, join(pt[2], first))

    def place(p, _):
        kvsend[p] = kvbuf[order[p]]
        return 0

    lax.fori_loop(0, BPS, place, 0)

    def kv_copy(o):
        to = ((sx + o // 4) % 4) * 4 + (sz + o % 4) % 4
        return remote(
            kvsend.at[pl.ds(2 * to, 2)], kv_hbm.at[pl.ds(2 * seq, 2)], ks_sem.at[o], kr_sem.at[o], to, head
        )

    def kv_arrival(o):
        source = ((sx + 4 - o // 4) % 4) * 4 + (sz + 4 - o % 4) % 4
        return remote(
            kvsend.at[pl.ds(2 * source, 2)], kv_hbm.at[pl.ds(2 * source, 2)], ks_sem.at[o], kr_sem.at[o], source, head
        )

    kv_own = pltpu.make_async_copy(kvsend.at[pl.ds(2 * seq, 2)], kv_hbm.at[pl.ds(2 * seq, 2)], kvl_sem)
    kv_own.start()
    for o in (4, 8, 12):
        kv_copy(o).start()

    g_copy(3, 0, gs_sem.at[0, 0], 1, znext).wait_recv()
    g_copy(3, 0, gs_sem.at[2, 0], 3, znext).start()
    g_copy(1, 1, gs_sem.at[0, 0], 2, znext).wait_recv()
    g_copy(1, 1, gs_sem.at[2, 1], 3, zprev).start()
    g_copy(3, 1, gs_sem.at[0, 0], 1, znext).wait_recv()
    g_copy(1, 0, gs_sem.at[0, 0], 2, znext).wait_recv()
    g_copy(2, 0, gs_sem.at[0, 0], 3, znext).wait_recv()
    g_copy(2, 1, gs_sem.at[0, 0], 3, znext).wait_recv()

    def bjoin(later, earlier):
        tmap, tshift = compose(later.astype(F32), earlier)
        return jnp.concatenate([tmap, tshift], axis=1)

    low = bjoin(gmap[1], gmap[0])
    total = join(bjoin(gmap[3], gmap[2]), low)
    srow[...] = total[:, 256:].astype(BF16)
    remote(srow, sin, hs_sem.at[0], hr_sem.at[0], xnext, head).start()

    for o in (1, 2, 3, 13, 14, 15):
        kv_copy(o).start()

    @pl.when(sz == 1)
    def _():
        pz[...] = gmap[0]

    @pl.when(sz == 2)
    def _():
        pz[...] = low.astype(BF16)

    @pl.when(sz == 3)
    def _():
        pz[...] = bjoin(gmap[2], low).astype(BF16)

    wprev, wnext = wo.at[((y + 3) % 4) * 2 + c], wo.at[((y + 1) % 4) * 2 + c]
    remote(wprev, wprev, ws_sem.at[1], wy_sem.at[1], seq, up).wait_recv()
    half = wo.at[((y + 3) % 4) * 2 + c, pl.ds(0, 64)]
    remote(half, half, ws_sem.at[3], wy_sem.at[3], seq, up).start()
    remote(wprev, wprev, ws_sem.at[5], wc_sem.at[1], seq, twin).start()
    remote(wnext, wnext, ws_sem.at[1], wy_sem.at[2], seq, up).wait_recv()
    half = wo.at[((y + 1) % 4) * 2 + c, pl.ds(64, 64)]
    remote(half, half, ws_sem.at[4], wy_sem.at[3], seq, down).start()
    remote(wnext, wnext, ws_sem.at[6], wc_sem.at[2], seq, twin).start()

    remote(srow, sin, hs_sem.at[0], hr_sem.at[0], xnext, head).wait_recv()
    ysend[...] = (mm(total[:, :256], sin[...]) + total[:, 256:]).astype(BF16)
    remote(ysend, xin, hs_sem.at[1], hr_sem.at[1], xnext, head).start()

    @pl.when(sz > 0)
    def _():
        def fold_all(p, _):
            fold(p, pz[...])
            return 0

        lax.fori_loop(0, 4, fold_all, 0)

    for o in (10, 9, 11):
        kv_copy(o).start()

    wfar = wo.at[((y + 2) % 4) * 2 + c]
    remote(wfar, wfar, ws_sem.at[1], wy_sem.at[3], seq, up).wait_recv()
    remote(wfar, wfar, ws_sem.at[7], wc_sem.at[3], seq, twin).start()

    remote(ysend, xin, hs_sem.at[1], hr_sem.at[1], xnext, head).wait_recv()
    enter = xin[...]

    def answer(j, rows):
        recalled = jnp.dot(rm[j, rows], enter, preferred_element_type=F32) + rs[j, rows]
        return unit(recalled).astype(BF16)

    def ret_copy(t, oy, oc):
        o, rows = oy * 2 + oc, pl.ds(t * HALF, HALF)
        to = ((y + oy) % 4) * 2 + (c + oc) % 2
        return remote(retsend.at[o, rows], ret.at[head, rows], as_sem.at[t, o], ar_sem.at[t, o], seq, to)

    def ret_arrival(t, oy, oc):
        o, rows = oy * 2 + oc, pl.ds(t * HALF, HALF)
        source = ((y + 4 - oy) % 4) * 2 + (c + oc) % 2
        return remote(retsend.at[o, rows], ret.at[source, rows], as_sem.at[t, o], ar_sem.at[t, o], seq, source)

    turns = [(2, 0), (2, 1), (1, 0), (1, 1), (3, 0), (3, 1), (0, 1)]
    for t in range(2):
        rows = pl.ds(t * HALF, HALF)
        for oy, oc in turns:
            retsend[oy * 2 + oc, rows] = answer(((y + oy) % 4) * 2 + (c + oc) % 2, rows)
            ret_copy(t, oy, oc).start()
        ret[head, rows] = answer(head, rows)
        if t == 0:
            for o in (5, 6, 7):
                kv_copy(o).start()

    for p, off in ((0, 0), (1, 3), (2, 1), (3, 2)):
        other = wo.at[((y + off) % 4) * 2 + 1 - c]
        remote(other, other, ws_sem.at[0], wc_sem.at[p], seq, twin).wait_recv()
    for load in loads:
        load.wait()
    for t in range(2):
        rows = slice(t * HALF, (t + 1) * HALF)
        total = tokens_ref[rows].astype(F32)
        for off in (0, 3, 1, 2):
            yp = (y + off) % 4
            if off > 0:
                ret_arrival(t, (4 - off) % 4, 0).wait_recv()
            ret_arrival(t, (4 - off) % 4, 1).wait_recv()
            left = jnp.concatenate([ret[2 * yp, rows], ret[2 * yp + 1, rows]], axis=1)
            total = total + jnp.dot(left, wo[pl.ds(2 * yp, 2)].reshape(2 * HD, D), preferred_element_type=F32)
        resid[rows] = total
        scale = lax.rsqrt(jnp.mean(total * total, axis=-1, keepdims=True) + EPS)
        ffn_in[rows] = (total * scale * fgain_ref[...]).astype(BF16)
        for i in range(FF // 256):
            cols = slice(i * 256, (i + 1) * 256)
            gate = jnp.dot(ffn_in[rows], wg[:, cols], preferred_element_type=F32)
            upper = jnp.dot(ffn_in[rows], wu[:, cols], preferred_element_type=F32)
            hid[rows, cols] = (gate / (1.0 + jnp.exp(-gate)) * upper).astype(BF16)
        for i in range(4):
            cols = slice(i * 256, (i + 1) * 256)
            down_part = jnp.dot(hid[rows], wd[:, cols], preferred_element_type=F32)
            mixed_ref[rows, cols] = (resid[rows, cols] + down_part).astype(BF16)

    def kv_end(o, _):
        kv_arrival(o).wait_recv()
        kv_copy(o).wait_send()
        return 0

    lax.fori_loop(1, 16, kv_end, 0)
    kv_own.wait()
    for i in range(4):
        y_copy(head, i, own_sem.at[0, i], 1, up).wait_send()
        y_copy(head, i, own_sem.at[1, i], 2, down).wait_send()
        y_copy(head, i, fwd_sem.at[i], 3, up).wait_send()
        for kind in range(4):
            twin_copy(head, i, kind).wait_send()
    for i in (0, 1, 2, 5, 6, 7):
        remote(wmine, wmine, ws_sem.at[i], wy_sem.at[1], seq, up).wait_send()
    half = wo.at[head, pl.ds(0, 64)]
    for i in (3, 4):
        remote(half, half, ws_sem.at[i], wy_sem.at[1], seq, up).wait_send()
    for i in range(2):
        for kind in range(3):
            g_copy(0, i, gs_sem.at[kind, i], 1, znext).wait_send()
    remote(srow, sin, hs_sem.at[0], hr_sem.at[0], xnext, head).wait_send()
    remote(ysend, xin, hs_sem.at[1], hr_sem.at[1], xnext, head).wait_send()
    for t in range(2):
        for oy, oc in turns:
            ret_copy(t, oy, oc).wait_send()


def settle_kernel(rowof_ref, mixed_in, kv_in, mixed_out, kv_out, sem, kv_sem):
    moves = [pltpu.make_async_copy(kv_in.at[i], kv_out.at[rowof_ref[i]], kv_sem.at[i]) for i in range(BPS)]
    moves.append(pltpu.make_async_copy(mixed_in, mixed_out, sem))
    for move in moves:
        move.start()
    for move in moves:
        move.wait()


def per_device(
    tokens, norm_gain, w_qkv, w_mem_gates, persist_keys, persist_values, alpha_bias, eta_bias,
    w_out, ffn_gain, w_gate, w_up, w_down, segment_ids, block_table,
):
    vmem = pl.BlockSpec(memory_space=pltpu.VMEM)
    smem = pl.BlockSpec(memory_space=pltpu.SMEM)
    anywhere = pl.BlockSpec(memory_space=pl.ANY)
    hbm = pl.BlockSpec(memory_space=pltpu.HBM)
    dma = pltpu.SemaphoreType.DMA
    mixed, arrived, rowof = pl.pallas_call(
        layer_kernel,
        out_shape=(
            jax.ShapeDtypeStruct((ROWS, D), BF16),
            jax.ShapeDtypeStruct((BPS, SPAN, 2 * HD), BF16),
            jax.ShapeDtypeStruct((BPS,), jnp.int32),
        ),
        in_specs=[smem] * 3 + [hbm] + [vmem] * 7 + [hbm] * 5,
        out_specs=(vmem, anywhere, smem),
        scratch_shapes=[
            pltpu.SMEM((BPS * SPAN,), jnp.int32),
            pltpu.SMEM((1024,), jnp.int32),
            pltpu.SMEM((BPS,), jnp.int32),
            pltpu.VMEM((D, 3 * HD), BF16),
            pltpu.VMEM((8, ROWS, D), BF16),
            pltpu.VMEM((8, HD, D), BF16),
            pltpu.VMEM((D, FF), BF16),
            pltpu.VMEM((D, FF), BF16),
            pltpu.VMEM((FF, D), BF16),
            pltpu.VMEM((BPS, SPAN, 2 * HD), BF16),
            pltpu.VMEM((BPS, SPAN, 2 * HD), BF16),
            pltpu.VMEM((8, ROWS, 2 * HD), BF16),
            pltpu.VMEM((8, ROWS, HD), F32),
            pltpu.VMEM((4, 2 * HD, 3 * HD), F32),
            pltpu.VMEM((4, 2 * HD, 3 * HD), BF16),
            pltpu.VMEM((2 * HD, 3 * HD), BF16),
            pltpu.VMEM((2 * HD, HD), BF16),
            pltpu.VMEM((2 * HD, HD), BF16),
            pltpu.VMEM((2 * HD, HD), BF16),
            pltpu.VMEM((2 * HD, HD), BF16),
            pltpu.VMEM((8, ROWS, HD), BF16),
            pltpu.VMEM((8, ROWS, HD), BF16),
            pltpu.VMEM((ROWS, D), F32),
            pltpu.VMEM((ROWS, D), BF16),
            pltpu.VMEM((ROWS, FF), BF16),
            dma((7,)), dma,
            dma((2, 4)), dma((4,)), dma((4, 4)), dma((4, 4)), dma((4, 4)),
            dma((8,)), dma((4,)), dma((4,)),
            dma((3, 2)), dma((4, 2)),
            dma((2,)), dma((2,)),
            dma((2, 8)), dma((2, 8)),
            dma((16,)), dma((16,)),
        ],
        compiler_params=pltpu.CompilerParams(
            collective_id=0, has_side_effects=True, vmem_limit_bytes=56 * MIB
        ),
    )(
        alpha_bias, eta_bias, block_table, segment_ids,
        block_table.reshape(4, 128), tokens, norm_gain.reshape(1, D), w_mem_gates.reshape(3, HD),
        persist_keys, persist_values, ffn_gain.reshape(1, D),
        w_qkv.reshape(D, 3 * HD), w_out, w_gate, w_up, w_down,
    )

    return pl.pallas_call(
        settle_kernel,
        out_shape=(
            jax.ShapeDtypeStruct((ROWS, D), BF16),
            jax.ShapeDtypeStruct((BPS, SPAN, 2 * HD), BF16),
        ),
        in_specs=[smem, vmem, vmem],
        out_specs=(hbm, hbm),
        scratch_shapes=[dma, dma((BPS,))],
    )(rowof, mixed, arrived)


def solution(mesh):
    return jax.shard_map(
        per_device,
        mesh=mesh,
        in_specs=(
            P(("seq", "head"), None),
            P(),
            P(None, "head", None),
            P("head", None, None),
            P(None, "head"),
            P(None, "head"),
            P("head"),
            P("head"),
            P("head", None),
            P(),
            P(),
            P(),
            P(),
            P(),
            P(),
        ),
        out_specs=(P(("seq", "head"), None), P("seq", None, "head")),
        check_vma=False,
    )
```

```python
import jax
import jax.numpy as jnp
from jax import lax
from jax.experimental import pallas as pl
from jax.experimental.pallas import tpu as pltpu
from jax.sharding import PartitionSpec as P

D = 1024
HD = 128
FF = 2816
PERS = 16
SPAN = 64
ROWS = 256
PIECE = 64
HALF = 128
TOKENS = 32768
BPS = 32
EPS = 1e-05
TINY = 1e-06
MIB = 1 << 20
MESH = pl.DeviceIdType.MESH
F32 = jnp.float32
BF16 = jnp.bfloat16


def sigmoid(x):
    return 1.0 / (1.0 + jnp.exp(-x))


def unit(x):
    return x * lax.rsqrt(jnp.mean(x * x, axis=-1, keepdims=True) + TINY)


def mm(a, b):
    return jnp.dot(a.astype(BF16), b.astype(BF16), preferred_element_type=F32)


def compose(later, earlier):
    joined = mm(later[:, :256], earlier)
    return joined[:, :256], joined[:, 256:] + later[:, 256:]


def layer_kernel(
    ab_ref, eb_ref, table_ref, ids_hbm,
    wide_table_ref, tokens_ref, ngain_ref, wmg_ref, pk_ref, pv_ref, fgain_ref,
    wq_hbm, wout_hbm, wg_hbm, wu_hbm, wd_hbm,
    mixed_ref, kv_hbm, rowof_ref,
    ids, before, order, wq_ref, xg, wo, wg, wu, wd, kvbuf, kvsend, rm, rs, pt, gmap, pz, srow, sin, ysend, xin,
    retsend, ret, resid, ffn_in, hid,
    local_sem, kvl_sem, own_sem, fwd_sem, tws_sem, yr_sem, twr_sem, ws_sem, wy_sem, wc_sem,
    gs_sem, gr_sem, hs_sem, hr_sem, as_sem, ar_sem, ks_sem, kr_sem,
):
    seq = lax.axis_index("seq")
    head = lax.axis_index("head")
    sx, sz = seq // 4, seq % 4
    y, c = head // 2, head % 2
    up = ((y + 1) % 4) * 2 + c
    down = ((y + 3) % 4) * 2 + c
    twin = y * 2 + (1 - c)
    znext = sx * 4 + (sz + 1) % 4
    zprev = sx * 4 + (sz + 3) % 4
    xnext = ((sx + 1) % 4) * 4 + sz

    def remote(src, dst, ssem, rsem, s, h):
        return pltpu.make_async_remote_copy(
            src_ref=src, dst_ref=dst, send_sem=ssem, recv_sem=rsem, device_id=(s, h), device_id_type=MESH
        )

    loads = [
        pltpu.make_async_copy(wg_hbm, wg, local_sem.at[0]),
        pltpu.make_async_copy(wu_hbm, wu, local_sem.at[1]),
        pltpu.make_async_copy(wd_hbm, wd, local_sem.at[2]),
    ]
    mine_ids = pl.multiple_of(seq * (BPS * SPAN), 1024)
    prior_ids = pl.multiple_of((seq * (BPS * SPAN) + TOKENS - 1024) % TOKENS, 1024)
    id_loads = [
        pltpu.make_async_copy(ids_hbm.at[pl.ds(mine_ids, BPS * SPAN)], ids, local_sem.at[3]),
        pltpu.make_async_copy(ids_hbm.at[pl.ds(prior_ids, 1024)], before, local_sem.at[4]),
    ]
    wq_load = pltpu.make_async_copy(wq_hbm, wq_ref, local_sem.at[5])
    wout_load = pltpu.make_async_copy(wout_hbm, wo.at[head], local_sem.at[6])
    for load in id_loads + [wq_load, wout_load]:
        load.start()

    barrier = pltpu.get_barrier_semaphore()

    def greet_head(o, _):
        pl.semaphore_signal(barrier, inc=1, device_id=(seq, (head + o) % 8), device_id_type=MESH)
        return 0

    def greet_seq(o, _):
        pl.semaphore_signal(barrier, inc=1, device_id=((seq + o) % 16, head), device_id_type=MESH)
        return 0

    lax.fori_loop(1, 8, greet_head, 0)
    lax.fori_loop(1, 16, greet_seq, 0)

    tok = tokens_ref[...].astype(F32)
    scale = lax.rsqrt(jnp.mean(tok * tok, axis=-1, keepdims=True) + EPS)
    xg[head] = (tok * scale * ngain_ref[...]).astype(BF16)

    pl.semaphore_wait(barrier, 22)

    def piece(slot, i):
        return xg.at[slot, pl.ds(i * PIECE, PIECE)]

    def y_copy(slot, i, sem, kind, to):
        part = piece(slot, i)
        return remote(part, part, sem, yr_sem.at[kind, i], seq, to)

    def twin_copy(slot, i, kind):
        part = piece(slot, i)
        return remote(part, part, tws_sem.at[kind, i], twr_sem.at[kind, i], seq, twin)

    slots = [2 * ((y + off) % 4) + c for off in (0, 3, 1, 2)]
    others = [2 * ((y + off) % 4) + 1 - c for off in (0, 3, 1, 2)]
    for i in range(4):
        y_copy(head, i, own_sem.at[0, i], 1, up).start()
        y_copy(head, 3 - i, own_sem.at[1, 3 - i], 2, down).start()
    for i in range(4):
        twin_copy(head, i, 0).start()
    for load in loads:
        load.start()

    initial = jnp.dot(
        pk_ref[...].astype(F32).T.astype(BF16), pv_ref[...], preferred_element_type=F32
    ) * (1.0 / PERS)
    row = lax.broadcasted_iota(jnp.int32, (HD, 3 * HD), 0)
    col = lax.broadcasted_iota(jnp.int32, (HD, 3 * HD), 1)
    eye_m = (row == col).astype(F32)
    eye_s = (row + HD == col).astype(F32)
    zero_wide = jnp.zeros((HD, 2 * HD), F32)
    fresh = jnp.concatenate([zero_wide, initial], axis=1)
    zero_rows = jnp.zeros((SPAN, 2 * HD), F32)

    wide = wide_table_ref[...]
    place_no = lax.broadcasted_iota(jnp.int32, (4, 128), 0) * 128 + lax.broadcasted_iota(jnp.int32, (4, 128), 1)
    owner_no = lax.shift_right_logical(wide, 5)
    key_no = owner_no * BPS + (place_no & (BPS - 1))
    position = jnp.zeros((4, 128), jnp.int32)
    for i in range(BPS):
        one = lax.shift_right_logical(table_ref[seq * BPS + i], 5) * BPS + i
        position = position + (one < key_no).astype(jnp.int32)
    position = jnp.where(lax.shift_right_logical(place_no, 5) == seq, position, -1)
    owned = (owner_no == seq).astype(F32)
    earlier = lax.broadcasted_iota(jnp.int32, (128, 128), 0) < lax.broadcasted_iota(jnp.int32, (128, 128), 1)
    rank = mm(jnp.concatenate([owned, owned], axis=0), earlier.astype(F32))[:4]
    rank = rank + 8.0 * lax.broadcasted_iota(jnp.int32, (4, 128), 0).astype(F32)
    rank = jnp.where(owned > 0.0, rank, -1.0)
    for i in range(BPS):
        order[i] = jnp.sum(jnp.where(position == i, place_no & (BPS - 1), 0))
        rowof_ref[i] = jnp.sum(jnp.where(rank == float(i), wide & (BPS - 1), 0))
    for load in id_loads:
        load.wait()

    def keep_of(yp, b):
        block = yp * 8 + b
        here = ids[block * SPAN]
        there = ids[jnp.maximum(block * SPAN - 1, 0)]
        there = jnp.where(block == 0, before[1023], there)
        there = jnp.where(block + seq == 0, -1, there)
        return jnp.where(here == there, 1.0, 0.0)

    def join(later, earlier):
        return jnp.concatenate(compose(later, earlier), axis=1)

    def project(x, first_block, yp):
        proj = jnp.dot(x, wq_ref[...], preferred_element_type=F32)
        q = unit(proj[:, :HD]) * HD ** (-0.5)
        k = unit(proj[:, HD : 2 * HD]) * HD ** (-0.5)
        v = proj[:, 2 * HD :]
        blocks = x.shape[0] // SPAN
        wmg = wmg_ref[...].astype(F32)
        theta = sigmoid(jnp.sum(v * wmg[0:1], axis=-1, keepdims=True)) * (1.0 / SPAN)
        mean_v = jnp.mean(v.reshape(blocks, SPAN, HD), axis=1)
        alpha = sigmoid(jnp.sum(mean_v * wmg[1:2], axis=-1, keepdims=True) + ab_ref[0])
        eta = sigmoid(jnp.sum(mean_v * wmg[2:3], axis=-1, keepdims=True) + eb_ref[0])
        qb, kb = q.astype(BF16), k.astype(BF16)
        kvbuf[pl.ds(yp * 8 + first_block, blocks), :, :HD] = kb.reshape(blocks, SPAN, HD)
        kvbuf[pl.ds(yp * 8 + first_block, blocks), :, HD:] = v.astype(BF16).reshape(blocks, SPAN, HD)
        return qb, k, kb, v, theta, alpha, eta

    def chains(work, steps):
        states = [[eye_m, eye_s, []] for _ in work]
        for step in range(steps):
            for (yp, block, at, (qb, k, kb, v, theta, alpha, eta)), state in zip(work, states):
                b = at + step
                rows = slice(b * SPAN, (b + 1) * SPAN)
                memory, moment, reads = state
                keep = keep_of(yp, block + step)
                held = keep * memory + (1.0 - keep) * fresh
                both = mm(jnp.concatenate([qb[rows], kb[rows]], axis=0), held)
                reads.append(both[:SPAN])
                wide_v = jnp.concatenate([zero_rows, v[rows]], axis=1)
                push = theta[rows] * (wide_v - both[SPAN:])
                moment = eta[b : b + 1] * (keep * moment) + mm(k[rows].T, push)
                state[0] = (1.0 - alpha[b : b + 1]) * held + moment
                state[1] = moment
        return [
            (jnp.concatenate(state[:2], axis=0), jnp.concatenate(state[2], axis=0)) for state in states
        ]

    def append(first, second):
        return join(second[0], first[0]), jnp.concatenate([first[1], join(second[1], first[0])], axis=0)

    def settle(yp, even, odd):
        tmap, reads = append(even, odd)
        pt[yp] = tmap
        rm[pl.ds(2 * yp, 2)] = reads[:, :256].astype(BF16).reshape(2, ROWS, 2 * HD)
        rs[pl.ds(2 * yp, 2)] = reads[:, 256:].reshape(2, ROWS, HD)

    def process(chips):
        work = []
        for yp in chips:
            made = project(xg[pl.ds(2 * yp, 2)].reshape(2 * ROWS, D), 0, yp)
            work += [(yp, 0, 0, made), (yp, 4, 4, made)]
        done = chains(work, 4)
        for i, yp in enumerate(chips):
            settle(yp, done[2 * i], done[2 * i + 1])

    def twin_in(kind):
        for i in range(4):
            twin_copy(others[kind], i, kind).wait_recv()

    wq_load.wait()
    wout_load.wait()
    twin_in(0)
    process([y])
    for i in range(4):
        y_copy(slots[1], i, own_sem.at[0, 0], 1, up).wait_recv()
        if i < 2:
            y_copy(slots[1], i, fwd_sem.at[i], 3, up).start()
        twin_copy(slots[1], i, 1).start()
        y_copy(slots[2], 3 - i, own_sem.at[0, 0], 2, up).wait_recv()
        if i < 2:
            y_copy(slots[2], 3 - i, fwd_sem.at[3 - i], 3, down).start()
        twin_copy(slots[2], 3 - i, 2).start()
    twin_in(1)
    twin_in(2)
    process([(y + 3) % 4, (y + 1) % 4])
    for i in (0, 3, 1, 2):
        y_copy(slots[3], i, own_sem.at[0, 0], 3, up).wait_recv()
        twin_copy(slots[3], i, 3).start()
    far = (y + 2) % 4
    here = project(xg[2 * far + c], 4 * c, far)
    twin_in(3)
    there = project(xg[2 * far + 1 - c], 4 * (1 - c), far)
    done = chains(
        [(far, 4 * c, 0, here), (far, 4 * c + 2, 2, here), (far, 4 - 4 * c, 0, there), (far, 6 - 4 * c, 2, there)], 2
    )
    here, there = append(done[0], done[1]), append(done[2], done[3])
    settle(
        far,
        [jnp.where(c == 0, a, b) for a, b in zip(here, there)],
        [jnp.where(c == 0, b, a) for a, b in zip(here, there)],
    )

    first = join(pt[1], pt[0])
    total = join(join(pt[3], pt[2]), first)
    gmap[sz] = total.astype(BF16)
    def g_copy(step, i, sem, kind, to):
        part = gmap.at[(sz + step) % 4, pl.ds(i * HD, HD)]
        return remote(part, part, sem, gr_sem.at[kind, i], to, head)

    for i in range(2):
        g_copy(0, i, gs_sem.at[0, i], 1, znext).start()
        g_copy(0, 1 - i, gs_sem.at[1, 1 - i], 2, zprev).start()

    wmine = wo.at[head]
    remote(wmine, wmine, ws_sem.at[1], wy_sem.at[1], seq, up).start()
    remote(wmine, wmine, ws_sem.at[2], wy_sem.at[2], seq, down).start()
    remote(wmine, wmine, ws_sem.at[0], wc_sem.at[0], seq, twin).start()

    def fold(p, emap):
        read = rm[pl.ds(2 * p, 2)].reshape(2 * ROWS, 2 * HD)
        out = jnp.dot(read, emap.astype(BF16), preferred_element_type=F32)
        rm[pl.ds(2 * p, 2)] = out[:, :256].astype(BF16).reshape(2, ROWS, 2 * HD)
        rs[pl.ds(2 * p, 2)] = rs[pl.ds(2 * p, 2)] + out[:, 256:].reshape(2, ROWS, HD)

    fold(1, pt[0])
    fold(2, first)
    fold(3, join(pt[2], first))

    def place(p, _):
        kvsend[p] = kvbuf[order[p]]
        return 0

    lax.fori_loop(0, BPS, place, 0)

    def kv_copy(o):
        to = ((sx + o // 4) % 4) * 4 + (sz + o % 4) % 4
        return remote(
            kvsend.at[pl.ds(2 * to, 2)], kv_hbm.at[pl.ds(2 * seq, 2)], ks_sem.at[o], kr_sem.at[o], to, head
        )

    def kv_arrival(o):
        source = ((sx + 4 - o // 4) % 4) * 4 + (sz + 4 - o % 4) % 4
        return remote(
            kvsend.at[pl.ds(2 * source, 2)], kv_hbm.at[pl.ds(2 * source, 2)], ks_sem.at[o], kr_sem.at[o], source, head
        )

    kv_own = pltpu.make_async_copy(kvsend.at[pl.ds(2 * seq, 2)], kv_hbm.at[pl.ds(2 * seq, 2)], kvl_sem)
    kv_own.start()
    for o in (4, 8, 12):
        kv_copy(o).start()

    g_copy(3, 0, gs_sem.at[0, 0], 1, znext).wait_recv()
    g_copy(3, 0, gs_sem.at[2, 0], 3, znext).start()
    g_copy(1, 1, gs_sem.at[0, 0], 2, znext).wait_recv()
    g_copy(1, 1, gs_sem.at[2, 1], 3, zprev).start()
    g_copy(3, 1, gs_sem.at[0, 0], 1, znext).wait_recv()
    g_copy(1, 0, gs_sem.at[0, 0], 2, znext).wait_recv()
    g_copy(2, 0, gs_sem.at[0, 0], 3, znext).wait_recv()
    g_copy(2, 1, gs_sem.at[0, 0], 3, znext).wait_recv()

    def bjoin(later, earlier):
        tmap, tshift = compose(later.astype(F32), earlier)
        return jnp.concatenate([tmap, tshift], axis=1)

    low = bjoin(gmap[1], gmap[0])
    total = join(bjoin(gmap[3], gmap[2]), low)
    srow[...] = total[:, 256:].astype(BF16)
    remote(srow, sin, hs_sem.at[0], hr_sem.at[0], xnext, head).start()

    for o in (13, 14, 15, 1, 2, 3):
        kv_copy(o).start()

    @pl.when(sz == 1)
    def _():
        pz[...] = gmap[0]

    @pl.when(sz == 2)
    def _():
        pz[...] = low.astype(BF16)

    @pl.when(sz == 3)
    def _():
        pz[...] = bjoin(gmap[2], low).astype(BF16)

    wprev, wnext = wo.at[((y + 3) % 4) * 2 + c], wo.at[((y + 1) % 4) * 2 + c]
    remote(wprev, wprev, ws_sem.at[1], wy_sem.at[1], seq, up).wait_recv()
    half = wo.at[((y + 3) % 4) * 2 + c, pl.ds(0, 64)]
    remote(half, half, ws_sem.at[3], wy_sem.at[3], seq, up).start()
    remote(wprev, wprev, ws_sem.at[5], wc_sem.at[1], seq, twin).start()
    remote(wnext, wnext, ws_sem.at[1], wy_sem.at[2], seq, up).wait_recv()
    half = wo.at[((y + 1) % 4) * 2 + c, pl.ds(64, 64)]
    remote(half, half, ws_sem.at[4], wy_sem.at[3], seq, down).start()
    remote(wnext, wnext, ws_sem.at[6], wc_sem.at[2], seq, twin).start()

    remote(srow, sin, hs_sem.at[0], hr_sem.at[0], xnext, head).wait_recv()
    ysend[...] = (mm(total[:, :256], sin[...]) + total[:, 256:]).astype(BF16)
    remote(ysend, xin, hs_sem.at[1], hr_sem.at[1], xnext, head).start()

    @pl.when(sz > 0)
    def _():
        def fold_all(p, _):
            fold(p, pz[...])
            return 0

        lax.fori_loop(0, 4, fold_all, 0)


    wfar = wo.at[((y + 2) % 4) * 2 + c]
    remote(wfar, wfar, ws_sem.at[1], wy_sem.at[3], seq, up).wait_recv()
    remote(wfar, wfar, ws_sem.at[7], wc_sem.at[3], seq, twin).start()

    remote(ysend, xin, hs_sem.at[1], hr_sem.at[1], xnext, head).wait_recv()
    enter = xin[...]

    def answer(j, rows):
        recalled = jnp.dot(rm[j, rows], enter, preferred_element_type=F32) + rs[j, rows]
        return unit(recalled).astype(BF16)

    def ret_copy(t, oy, oc):
        o, rows = oy * 2 + oc, pl.ds(t * HALF, HALF)
        to = ((y + oy) % 4) * 2 + (c + oc) % 2
        return remote(retsend.at[o, rows], ret.at[head, rows], as_sem.at[t, o], ar_sem.at[t, o], seq, to)

    def ret_arrival(t, oy, oc):
        o, rows = oy * 2 + oc, pl.ds(t * HALF, HALF)
        source = ((y + 4 - oy) % 4) * 2 + (c + oc) % 2
        return remote(retsend.at[o, rows], ret.at[source, rows], as_sem.at[t, o], ar_sem.at[t, o], seq, source)

    turns = [(2, 0), (2, 1), (1, 0), (1, 1), (3, 0), (3, 1), (0, 1)]
    for t in range(2):
        rows = pl.ds(t * HALF, HALF)
        for oy, oc in turns:
            retsend[oy * 2 + oc, rows] = answer(((y + oy) % 4) * 2 + (c + oc) % 2, rows)
            ret_copy(t, oy, oc).start()
        ret[head, rows] = answer(head, rows)
        if t == 0:
            for o in (10, 9, 11, 5, 6, 7):
                kv_copy(o).start()

    for p, off in ((0, 0), (1, 3), (2, 1), (3, 2)):
        other = wo.at[((y + off) % 4) * 2 + 1 - c]
        remote(other, other, ws_sem.at[0], wc_sem.at[p], seq, twin).wait_recv()
    for load in loads:
        load.wait()
    for t in range(2):
        rows = slice(t * HALF, (t + 1) * HALF)
        total = tokens_ref[rows].astype(F32)
        for off in (0, 3, 1, 2):
            yp = (y + off) % 4
            if off > 0:
                ret_arrival(t, (4 - off) % 4, 0).wait_recv()
            ret_arrival(t, (4 - off) % 4, 1).wait_recv()
            left = jnp.concatenate([ret[2 * yp, rows], ret[2 * yp + 1, rows]], axis=1)
            total = total + jnp.dot(left, wo[pl.ds(2 * yp, 2)].reshape(2 * HD, D), preferred_element_type=F32)
        resid[rows] = total
        scale = lax.rsqrt(jnp.mean(total * total, axis=-1, keepdims=True) + EPS)
        ffn_in[rows] = (total * scale * fgain_ref[...]).astype(BF16)
        for i in range(FF // 256):
            cols = slice(i * 256, (i + 1) * 256)
            gate = jnp.dot(ffn_in[rows], wg[:, cols], preferred_element_type=F32)
            upper = jnp.dot(ffn_in[rows], wu[:, cols], preferred_element_type=F32)
            hid[rows, cols] = (gate / (1.0 + jnp.exp(-gate)) * upper).astype(BF16)
        for i in range(4):
            cols = slice(i * 256, (i + 1) * 256)
            down_part = jnp.dot(hid[rows], wd[:, cols], preferred_element_type=F32)
            mixed_ref[rows, cols] = (resid[rows, cols] + down_part).astype(BF16)

    def kv_end(o, _):
        kv_arrival(o).wait_recv()
        kv_copy(o).wait_send()
        return 0

    lax.fori_loop(1, 16, kv_end, 0)
    kv_own.wait()
    for i in range(4):
        y_copy(head, i, own_sem.at[0, i], 1, up).wait_send()
        y_copy(head, i, own_sem.at[1, i], 2, down).wait_send()
        y_copy(head, i, fwd_sem.at[i], 3, up).wait_send()
        for kind in range(4):
            twin_copy(head, i, kind).wait_send()
    for i in (0, 1, 2, 5, 6, 7):
        remote(wmine, wmine, ws_sem.at[i], wy_sem.at[1], seq, up).wait_send()
    half = wo.at[head, pl.ds(0, 64)]
    for i in (3, 4):
        remote(half, half, ws_sem.at[i], wy_sem.at[1], seq, up).wait_send()
    for i in range(2):
        for kind in range(3):
            g_copy(0, i, gs_sem.at[kind, i], 1, znext).wait_send()
    remote(srow, sin, hs_sem.at[0], hr_sem.at[0], xnext, head).wait_send()
    remote(ysend, xin, hs_sem.at[1], hr_sem.at[1], xnext, head).wait_send()
    for t in range(2):
        for oy, oc in turns:
            ret_copy(t, oy, oc).wait_send()


def settle_kernel(rowof_ref, mixed_in, kv_in, mixed_out, kv_out, sem, kv_sem):
    moves = [pltpu.make_async_copy(kv_in.at[i], kv_out.at[rowof_ref[i]], kv_sem.at[i]) for i in range(BPS)]
    moves.append(pltpu.make_async_copy(mixed_in, mixed_out, sem))
    for move in moves:
        move.start()
    for move in moves:
        move.wait()


def per_device(
    tokens, norm_gain, w_qkv, w_mem_gates, persist_keys, persist_values, alpha_bias, eta_bias,
    w_out, ffn_gain, w_gate, w_up, w_down, segment_ids, block_table,
):
    vmem = pl.BlockSpec(memory_space=pltpu.VMEM)
    smem = pl.BlockSpec(memory_space=pltpu.SMEM)
    anywhere = pl.BlockSpec(memory_space=pl.ANY)
    hbm = pl.BlockSpec(memory_space=pltpu.HBM)
    dma = pltpu.SemaphoreType.DMA
    mixed, arrived, rowof = pl.pallas_call(
        layer_kernel,
        out_shape=(
            jax.ShapeDtypeStruct((ROWS, D), BF16),
            jax.ShapeDtypeStruct((BPS, SPAN, 2 * HD), BF16),
            jax.ShapeDtypeStruct((BPS,), jnp.int32),
        ),
        in_specs=[smem] * 3 + [hbm] + [vmem] * 7 + [hbm] * 5,
        out_specs=(vmem, anywhere, smem),
        scratch_shapes=[
            pltpu.SMEM((BPS * SPAN,), jnp.int32),
            pltpu.SMEM((1024,), jnp.int32),
            pltpu.SMEM((BPS,), jnp.int32),
            pltpu.VMEM((D, 3 * HD), BF16),
            pltpu.VMEM((8, ROWS, D), BF16),
            pltpu.VMEM((8, HD, D), BF16),
            pltpu.VMEM((D, FF), BF16),
            pltpu.VMEM((D, FF), BF16),
            pltpu.VMEM((FF, D), BF16),
            pltpu.VMEM((BPS, SPAN, 2 * HD), BF16),
            pltpu.VMEM((BPS, SPAN, 2 * HD), BF16),
            pltpu.VMEM((8, ROWS, 2 * HD), BF16),
            pltpu.VMEM((8, ROWS, HD), F32),
            pltpu.VMEM((4, 2 * HD, 3 * HD), F32),
            pltpu.VMEM((4, 2 * HD, 3 * HD), BF16),
            pltpu.VMEM((2 * HD, 3 * HD), BF16),
            pltpu.VMEM((2 * HD, HD), BF16),
            pltpu.VMEM((2 * HD, HD), BF16),
            pltpu.VMEM((2 * HD, HD), BF16),
            pltpu.VMEM((2 * HD, HD), BF16),
            pltpu.VMEM((8, ROWS, HD), BF16),
            pltpu.VMEM((8, ROWS, HD), BF16),
            pltpu.VMEM((ROWS, D), F32),
            pltpu.VMEM((ROWS, D), BF16),
            pltpu.VMEM((ROWS, FF), BF16),
            dma((7,)), dma,
            dma((2, 4)), dma((4,)), dma((4, 4)), dma((4, 4)), dma((4, 4)),
            dma((8,)), dma((4,)), dma((4,)),
            dma((3, 2)), dma((4, 2)),
            dma((2,)), dma((2,)),
            dma((2, 8)), dma((2, 8)),
            dma((16,)), dma((16,)),
        ],
        compiler_params=pltpu.CompilerParams(
            collective_id=0, has_side_effects=True, vmem_limit_bytes=56 * MIB
        ),
    )(
        alpha_bias, eta_bias, block_table, segment_ids,
        block_table.reshape(4, 128), tokens, norm_gain.reshape(1, D), w_mem_gates.reshape(3, HD),
        persist_keys, persist_values, ffn_gain.reshape(1, D),
        w_qkv.reshape(D, 3 * HD), w_out, w_gate, w_up, w_down,
    )

    return pl.pallas_call(
        settle_kernel,
        out_shape=(
            jax.ShapeDtypeStruct((ROWS, D), BF16),
            jax.ShapeDtypeStruct((BPS, SPAN, 2 * HD), BF16),
        ),
        in_specs=[smem, vmem, vmem],
        out_specs=(hbm, hbm),
        scratch_shapes=[dma, dma((BPS,))],
    )(rowof, mixed, arrived)


def solution(mesh):
    return jax.shard_map(
        per_device,
        mesh=mesh,
        in_specs=(
            P(("seq", "head"), None),
            P(),
            P(None, "head", None),
            P("head", None, None),
            P(None, "head"),
            P(None, "head"),
            P("head"),
            P("head"),
            P("head", None),
            P(),
            P(),
            P(),
            P(),
            P(),
            P(),
        ),
        out_specs=(P(("seq", "head"), None), P("seq", None, "head")),
        check_vma=False,
    )
```
